256 devices in a mesh: rows: 64 (over y, z, core), feat: 4 (over x).
Axes of the slice: x: 4, y: 4, z: 8, core: 2. Of those that a mesh axis runs over, the one named last changes fastest.
Arguments:
- gradients: bfloat16 [32768, 128], P('rows'), may hold values from -6 to 6
- hessians: bfloat16 [32768], P('rows'), may hold values from 0.25 to 2
- bin_words: int32 [128, 32768], P('feat', 'rows'), may hold values from 0 to 4095, as said below
- children: int32 [3, 32768], P(None, 'rows'), may hold values from 0 to 1, as said below
- split_feature: int32 [14], replicated, may hold values from 0 to 255
- split_bin: int32 [14], replicated, may hold values from 0 to 62
Outputs:
- split_gain_one: float32 [128, 256], P('rows', 'feat')
- split_gain_two: float32 [256, 256], P('rows', 'feat')
- split_gain_three: float32 [512, 256], P('rows', 'feat')
- child_scores: float32 [3, 64, 2, 128], P(None, 'rows')
The draws below stay inside these ranges and needn't reach their ends.
Inputs may be any that keep to these rules, and one draw needn't show every extreme that they name: `children`: of the 512 rows of one device, at most 3 / 4, 1 / 2 and 1 / 4 of 512 lie in one node at depths 1, 2 and 3; every device reaches each of these bounds in some node. `bin_words`: word w of panel p, six bits a feature with the lowest bits first, holds the bins of the panel's features 2 w and 2 w + 1, numbered within the panel of 64 features; slots past the panel's last feature are zero. Every bin is below 64.
All inputs are finite; a program needn't handle non-finite values.
Results may differ from the reference program's by a relative error of at most 0.0003.
Values may be sent and summed in bfloat16 or wider, within the bound.
A program may use at most 64 MiB of HBM per device.

```python
import math
import jax
import jax.numpy as jnp
from jax import lax

FEATURES = 256
BINS = 64
OUT = 128
LEVELS = 3
ROW_DEV = 512
ROWS_TOTAL = 32768
SPLITS = 14
N_ROWS = 64
N_FEAT = 4


def draw_bin_words(key, part):
    feat_dev = FEATURES // N_FEAT
    words_dev = (feat_dev + 1) // 2
    bin_codes = jax.random.randint(key, (N_FEAT, words_dev * 2, ROWS_TOTAL), 0, BINS, dtype=jnp.int32)
    in_panel = (jnp.arange(words_dev * 2) < feat_dev).astype(jnp.int32)
    bin_codes = bin_codes * in_panel[None, :, None]
    shifts = 6 * jnp.arange(2, dtype=jnp.int32)
    packed = jnp.sum(jnp.left_shift(bin_codes.reshape(N_FEAT, words_dev, 2, ROWS_TOTAL), shifts[None, None, :, None]), axis=2)
    return packed.reshape(N_FEAT * words_dev, ROWS_TOTAL).astype(jnp.int32)


def draw_children(key, part):
    flip_key = jax.random.fold_in(key, 11)
    order_key = jax.random.fold_in(key, 23)
    flip_bits = jax.random.randint(flip_key, (N_ROWS, 7), 0, 2, dtype=jnp.int32)
    unit_rows = ROW_DEV // 64
    leaf_table = jnp.array([1, 3, 4, 8, 4, 12, 16, 16], jnp.int32) * unit_rows
    leaf_bounds = jnp.cumsum(leaf_table)[:7]
    positions = jnp.arange(ROW_DEV, dtype=jnp.int32)
    leaf_sorted = jnp.sum((positions[:, None] >= leaf_bounds[None, :]).astype(jnp.int32), axis=1)
    row_orders = jax.vmap(lambda sub_key: jax.random.permutation(sub_key, ROW_DEV))(jax.random.split(order_key, N_ROWS))
    leaf_rows = leaf_sorted[row_orders]
    heavy_top = jnp.bitwise_and(jnp.right_shift(leaf_rows, 2), 1)
    heavy_mid = jnp.bitwise_and(jnp.right_shift(leaf_rows, 1), 1)
    heavy_low = jnp.bitwise_and(leaf_rows, 1)
    child_top = jnp.bitwise_xor(heavy_top, flip_bits[:, 0:1])
    child_mid = jnp.bitwise_xor(heavy_mid, jnp.take_along_axis(flip_bits[:, 1:3], child_top, axis=1))
    node_mid = child_top * 2 + child_mid
    child_low = jnp.bitwise_xor(heavy_low, jnp.take_along_axis(flip_bits[:, 3:7], node_mid, axis=1))
    return jnp.stack([child_top, child_mid, child_low], 0).reshape(3, N_ROWS * ROW_DEV).astype(jnp.int32)


def touch_ends(entries, stream_key, low, high):
    longest = entries.shape.index(max(entries.shape))
    spots = []
    for shift in (0, 1):
        where = [jax.random.randint(jax.random.fold_in(stream_key, axis), (), 0, length) for axis, length in enumerate(entries.shape)]
        where[longest] = (where[longest] + shift) % entries.shape[longest]
        spots.append(tuple(where))
    return entries.at[spots[0]].set(low).at[spots[1]].set(high)


def block_levels(rng, shape, cuts, smallest, top_value):
    gain, own = 1.0, jax.random.fold_in(rng, 6)
    for dim, parts in cuts:
        steps = jnp.exp(jax.random.uniform(jax.random.fold_in(own, dim), (parts,), jnp.float32, smallest / len(cuts), top_value / len(cuts)))
        gain = gain * jnp.repeat(steps, shape[dim] // parts).reshape([-1 if axis == dim else 1 for axis in range(len(shape))])
    return gain


def centred(own_key, dims, width, most, shards=(), kind=jnp.bfloat16):
    result = width * jax.random.normal(own_key, dims, jnp.float32)
    if shards:
        result = result * block_levels(own_key, dims, shards, -0.22, 0.18)
    return jnp.clip(result, -most, most).astype(kind)


def setup_inputs(seed: int = 0) -> dict:
    key_of = jax.random.split(jax.random.key(seed), 7)
    return {
        "gradients": centred(key_of[0], (ROWS_TOTAL, OUT), 1.0, 6.0, ((0, 64),)),
        "hessians": jnp.clip(jnp.exp(math.log(2.0) - 2.0794415 * jax.random.uniform(key_of[1], (ROWS_TOTAL,), jnp.float32) ** block_levels(key_of[1], (ROWS_TOTAL,), ((0, 64),), -0.2, 0.2)), 0.25, 2.0).astype(jnp.bfloat16),
        "bin_words": draw_bin_words(jax.random.fold_in(key_of[6], 71), 0),
        "children": draw_children(jax.random.fold_in(key_of[6], 71), 0),
        "split_feature": touch_ends(jax.random.randint(key_of[4], (SPLITS,), 0, FEATURES), jax.random.fold_in(key_of[4], 1), 0, FEATURES - 1).astype(jnp.int32),
        "split_bin": touch_ends(jax.random.randint(key_of[5], (SPLITS,), 0, BINS - 1), jax.random.fold_in(key_of[5], 1), 0, (BINS - 1) - 1).astype(jnp.int32),
    }


penalty = 1.0

def unpack_codes(packed, feat_count):
    shifts = 6 * jnp.arange(2, dtype=jnp.int32)
    pieces = jnp.bitwise_and(jnp.right_shift(packed[:, None, :], shifts[None, :, None]), 63)
    return pieces.reshape(-1, packed.shape[-1])[:feat_count]

def split_terms(cumulative, hess_cum):
    total_sum = cumulative[..., -1:, :]
    hess_total = hess_cum[..., -1:]
    right_sum = total_sum - cumulative
    hess_right = hess_total - hess_cum
    split_score = (lax.optimization_barrier(jnp.sum(cumulative * cumulative, -1)) / (hess_cum + penalty) + lax.optimization_barrier(jnp.sum(right_sum * right_sum, -1)) / (hess_right + penalty) - lax.optimization_barrier(jnp.sum(total_sum * total_sum, -1)) / (hess_total + penalty)) / OUT
    return (split_score, right_sum, hess_right)

def reference(gradients, hessians, bin_words, children, split_feature, split_bin):
    feat_dev = FEATURES // N_FEAT
    words_dev = bin_words.shape[0] // N_FEAT
    bin_codes = jnp.concatenate([unpack_codes(bin_words[panel_index * words_dev:(panel_index + 1) * words_dev], feat_dev) for panel_index in range(N_FEAT)], 0)
    grad_wide = gradients.astype(jnp.float32)
    hess_wide = hessians.astype(jnp.float32)
    node_ids = jnp.zeros((gradients.shape[0],), jnp.int32)
    gain_list = []
    score_list = []
    for level_index in range(LEVELS):
        node_ids = node_ids * 2 + children[level_index].astype(jnp.int32)
        node_count = 2 ** (level_index + 1)

        def one_feature(code_row):
            segment = node_ids * BINS + code_row
            return (jax.ops.segment_sum(grad_wide, segment, node_count * BINS), jax.ops.segment_sum(hess_wide, segment, node_count * BINS))
        hist_grad, hist_hess = lax.map(one_feature, bin_codes)
        hist_grad = hist_grad.reshape(FEATURES, node_count, BINS, OUT)
        hist_hess = hist_hess.reshape(FEATURES, node_count, BINS)
        cumulative = jnp.cumsum(hist_grad, axis=2)
        hess_cum = jnp.cumsum(hist_hess, axis=2)
        split_score, right_sum, hess_right = split_terms(cumulative, hess_cum)
        gain_list.append(split_score.reshape(N_FEAT, feat_dev, node_count, BINS).transpose(2, 1, 0, 3).reshape(node_count * feat_dev, N_FEAT * BINS))
        first_slot = node_count - 2
        feature_ids = split_feature[first_slot:first_slot + node_count]
        bin_ids = split_bin[first_slot:first_slot + node_count]
        node_range = jnp.arange(node_count, dtype=jnp.int32)
        left_grad = cumulative[feature_ids, node_range, bin_ids]
        left_hess = hess_cum[feature_ids, node_range, bin_ids]
        right_grad = right_sum[feature_ids, node_range, bin_ids]
        right_hess = hess_right[feature_ids, node_range, bin_ids]
        child_pair = jnp.stack([-left_grad / jnp.sqrt(left_hess + penalty)[:, None], -right_grad / jnp.sqrt(right_hess + penalty)[:, None]], 1)
        score_list.append(jnp.repeat(child_pair, N_ROWS // node_count, axis=0))
    return (gain_list[0], gain_list[1], gain_list[2], jnp.stack(score_list, 0))
```

```python
import jax
import jax.numpy as jnp
from jax import lax
from jax.experimental import pallas as pl
from jax.experimental.pallas import tpu as pltpu
from jax.sharding import PartitionSpec as P

BINS = 64
OUT = 128
SPLITS = 14
ROW_DEV = 512
SLOTS = 128
NY, NZ, NX = 4, 8, 4
HEAD = 144
ROWS_ALL = HEAD + 64
ROWS_DST = HEAD + 16
KEEP = 136
MESH = pl.DeviceIdType.MESH
F32 = jnp.float32
BF16 = jnp.bfloat16

penalty = 1.0
ZZ_ORDER = (0, 3, 1, 2)


def gray(two_bits):
    return two_bits + (two_bits // 2) * (5 - 2 * two_bits)


def block_of(y, parity):
    block = 2 * (((y + 1) // 2) % 2) + y // 2
    return block + parity * (3 - 2 * block)


def nt_dot(left, right):
    return lax.dot_general(left, right, (((1,), (1,)), ((), ())), preferred_element_type=F32)


def gains_of(left):
    total = jnp.broadcast_to(left[:, 127:128], left.shape)
    right = total - left

    def term(part):
        square = part[:OUT] * part[:OUT]
        return jnp.sum(square, axis=0, keepdims=True) / (part[OUT:OUT + 1] + penalty)

    return (term(left) + term(right) - term(total)) / OUT


def kernel(
    split_feature, split_bin, grad_ref, hess_ref, word_ref, child_ref,
    one_ref, two_ref, three_ref, child_out,
    feed, sent, got_z, got_y, acc, half, deep, sib, mid, low,
    gain3, home3, gain2, home2, part, part_y, mine_z, part_z, mine_x, part_x,
    z_send, z_recv, y_send, y_recv, core_send, core_recv, sib_send, sib_recv,
    low_send, low_recv, g3_send, g3_recv, g2_send, g2_recv,
    py_send, py_recv, pz_send, pz_recv, px_send, px_recv,
):
    row = lax.axis_index("rows")
    x = lax.axis_index("feat")
    core = row % 2
    z = (row // 2) % NZ
    y = row // 16
    parity = z % 2
    order = gray(z // 2)
    node = 4 * parity + order
    bit0 = order % 2
    bit1 = order // 2
    block = block_of(y, parity)

    def at(y_to, z_to, core_to):
        return y_to * 16 + z_to * 2 + core_to

    def remote(src, dst, send, recv, row_to, x_to=None):
        return pltpu.make_async_remote_copy(
            src_ref=src, dst_ref=dst, send_sem=send, recv_sem=recv,
            device_id=(row_to, x if x_to is None else x_to), device_id_type=MESH,
        )

    def arrived(ref, sem):
        pltpu.make_async_copy(ref, ref, sem).wait()

    barrier = pltpu.get_barrier_semaphore()

    def greet(row_to, x_to):
        pl.semaphore_signal(barrier, inc=1, device_id=(row_to, x_to), device_id_type=MESH)

    for step in range(1, NZ):
        greet(at(y, (z + step) % NZ, core), x)
    for step in range(1, NY):
        greet(at((y + step) % NY, z, core), x)
    for step in range(1, 2 * NX):
        greet(at(y, z, (core + step) % 2), (x + step // 2) % NX)

    child = child_ref[...]
    node1 = child[0:1]
    node2 = node1 * 2 + child[1:2]
    node3 = node2 * 2 + child[2:3]
    at_node = (lax.broadcasted_iota(jnp.int32, (8, ROW_DEV), 0) == node3).astype(F32)
    upto = (
        lax.broadcasted_iota(jnp.int32, (ROW_DEV, ROW_DEV), 0)
        <= lax.broadcasted_iota(jnp.int32, (ROW_DEV, ROW_DEV), 1)
    ).astype(F32).astype(BF16)
    running = jnp.dot(at_node.astype(BF16), upto, preferred_element_type=F32)
    rank = jnp.sum(at_node * running, axis=0, keepdims=True).astype(jnp.int32) - 1
    low_bits = jnp.bitwise_and(node3, 3)
    node_z = 2 * jnp.bitwise_xor(low_bits, jnp.right_shift(low_bits, 1)) + jnp.right_shift(node3, 2)
    slot = node_z * SLOTS + rank

    hess = hess_ref[...].astype(F32)
    feed[0:OUT, :] = grad_ref[...].astype(F32).T.astype(BF16)
    feed[OUT:HEAD, :] = jnp.concatenate(
        [hess, jnp.zeros((HEAD - OUT - 1, ROW_DEV), F32)], 0
    ).astype(BF16)
    words = word_ref[...]
    natural = jnp.concatenate(
        [jnp.bitwise_and(words, 63), jnp.bitwise_and(jnp.right_shift(words, 6), 63)], 0
    ).astype(F32).astype(BF16)
    spot64 = lax.broadcasted_iota(jnp.int32, (64, 1), 0)
    source64 = (
        32 * jnp.bitwise_and(jnp.right_shift(spot64, 3), 1)
        + 16 * jnp.right_shift(spot64, 5)
        + 2 * jnp.bitwise_and(spot64, 7)
        + jnp.bitwise_and(jnp.right_shift(spot64, 4), 1)
    )
    moved = (lax.broadcasted_iota(jnp.int32, (64, 64), 1) == source64).astype(F32).astype(BF16)
    feed[HEAD:ROWS_ALL, :] = jnp.dot(moved, natural, preferred_element_type=F32).astype(BF16)

    packed = feed[...]
    pl.semaphore_wait(barrier, (NZ - 1) + (NY - 1) + (2 * NX - 1))
    for pair in range(NZ // 2):
        wanted = lax.broadcasted_iota(jnp.int32, (2 * SLOTS, ROW_DEV), 0) + pair * 2 * SLOTS
        pick = (wanted == slot).astype(F32).astype(BF16)
        chosen = nt_dot(packed, pick).astype(BF16)
        for side in range(2):
            z_to = 2 * pair + side
            sent[z_to] = chosen[:, side * SLOTS:(side + 1) * SLOTS]

            @pl.when(z_to != z)
            def _(z_to=z_to):
                remote(
                    sent.at[z_to], got_z.at[z], z_send.at[z_to], z_recv.at[z], at(y, z_to, core)
                ).start()

            @pl.when(z_to == z)
            def _(z_to=z_to):
                pltpu.make_async_copy(sent.at[z_to], got_z.at[z], z_recv.at[z]).start()

    rows32 = lax.broadcasted_iota(jnp.int32, (32, 1), 0)
    yy = jnp.right_shift(rows32, 3)
    which = jnp.bitwise_and(jnp.right_shift(rows32, 1), 3)
    right_side = jnp.bitwise_and(rows32, 1)
    is_one, is_two = which == 0, which == 1
    node_row = jnp.where(
        is_one, jnp.right_shift(yy, 1), jnp.where(is_two, yy, 2 * yy + which - 2)
    )
    split_row = node_row + jnp.where(is_one, 0, jnp.where(is_two, 2, 6))
    feature_row = jnp.zeros((32, 1), jnp.int32)
    bin_row = jnp.zeros((32, 1), jnp.int32)
    for s in range(SPLITS):
        feature_row = jnp.where(split_row == s, split_feature[s], feature_row)
        bin_row = jnp.where(split_row == s, split_bin[s], bin_row)
    inner = jnp.bitwise_and(feature_row, 63)
    place = (
        32 * jnp.right_shift(inner, 5)
        + 16 * jnp.bitwise_and(jnp.right_shift(inner, 1), 1)
        + 8 * jnp.bitwise_and(inner, 1)
        + jnp.bitwise_and(jnp.right_shift(inner, 2), 7)
    )
    panel_row = jnp.right_shift(feature_row, 6)
    spot = (lax.broadcasted_iota(jnp.int32, (32, 64), 1) == place).astype(F32).astype(BF16)
    code_row = jnp.dot(spot, feed[HEAD:ROWS_ALL, :], preferred_element_type=F32).astype(jnp.int32)
    node_here = jnp.where(is_one, node1, jnp.where(is_two, node2, node3))
    goes_right = (code_row > bin_row).astype(jnp.int32)
    wanted_row = (node_here == node_row) & (panel_row == x) & (goes_right == right_side)
    wanted_row = wanted_row.astype(F32)
    sums = jnp.dot(wanted_row.astype(BF16), grad_ref[...], preferred_element_type=F32)
    sums_h = jnp.sum(wanted_row * hess, axis=1, keepdims=True)
    for y_to in range(NY):
        part[y_to, 0:8] = sums[8 * y_to:8 * y_to + 8]
        part[y_to, 8:16] = jnp.broadcast_to(sums_h[8 * y_to:8 * y_to + 8], (8, OUT))
    acc[...] = jnp.zeros_like(acc)
    for step in range(1, NY):
        y_to = (y + step) % NY
        remote(
            part.at[y_to], part_y.at[y], py_send.at[step], py_recv.at[y], at(y_to, z, core)
        ).start()
    pltpu.make_async_copy(part.at[y], part_y.at[y], py_recv.at[y]).start()

    for step in (0, 1, 7, 2, 6, 3, 5, 4):
        z_from = (z + step) % NZ
        arrived(got_z.at[z_from], z_recv.at[z_from])
        for y_step in (1, 3, 2):
            y_to = (y + y_step) % NY
            start = pl.multiple_of(HEAD + 16 * block_of(y_to, parity), 16)
            remote(
                got_z.at[z_from, pl.ds(0, HEAD)], got_y.at[y, z_from, pl.ds(0, HEAD)],
                y_send.at[y_step], y_recv.at[y], at(y_to, z, core),
            ).start()
            remote(
                got_z.at[z_from, pl.ds(start, 16)], got_y.at[y, z_from, pl.ds(HEAD, 16)],
                y_send.at[y_step], y_recv.at[y], at(y_to, z, core),
            ).start()
        start = pl.multiple_of(HEAD + 16 * block, 16)
        pltpu.make_async_copy(
            got_z.at[z_from, pl.ds(0, HEAD)], got_y.at[y, z_from, pl.ds(0, HEAD)], y_recv.at[y]
        ).start()
        pltpu.make_async_copy(
            got_z.at[z_from, pl.ds(start, 16)], got_y.at[y, z_from, pl.ds(HEAD, 16)], y_recv.at[y]
        ).start()

    for y_from in range(NY):
        arrived(part_y.at[y_from], py_recv.at[y_from])
    mine_z[...] = (part_y[0] + part_y[1]) + (part_y[2] + part_y[3])

    bins = lax.broadcasted_iota(jnp.int32, (BINS, 1), 0).astype(F32)

    def add_rows(step, carry):
        y_from = (y + gray(step)) % NY
        arrived(got_y.at[y_from], y_recv.at[y_from])
        values = jnp.concatenate([got_y[y_from, i, 0:HEAD, :] for i in range(NZ)], 1)
        codes = jnp.concatenate(
            [got_y[y_from, i, HEAD:ROWS_DST, :] for i in range(NZ)], 1
        ).astype(F32)
        for pair in range(4):
            masks = []
            for place_index in (2 * (pair % 2), 2 * (pair % 2) + 1):
                zh = 2 * ZZ_ORDER[place_index] + pair // 2
                for i in (zh, 8 + zh):
                    masks.append((codes[i:i + 1] <= bins).astype(F32).astype(BF16))
            found = nt_dot(values, jnp.concatenate(masks, 0))
            acc[2 * pair] += found[:KEEP, 0:128]
            acc[2 * pair + 1] += found[:KEEP, 128:256]
        return carry

    lax.fori_loop(0, NY, add_rows, 0)

    own = 2 * bit0
    other = 2 * (1 - bit0)
    buddy = at(y, z, 1 - core)
    for turn, first_place in ((0, other), (1, own)):
        remote(
            acc.at[pl.ds(4 * (1 - core) + first_place, 2)], half.at[pl.ds(first_place, 2)],
            core_send.at[turn], core_recv.at[turn], buddy,
        ).start()

    for step in range(1, NZ):
        remote(
            mine_z, part_z.at[z], pz_send.at[step], pz_recv.at[z], at(y, (z + step) % NZ, core)
        ).start()
    pltpu.make_async_copy(mine_z, part_z.at[z], pz_recv.at[z]).start()

    arrived(half.at[pl.ds(other, 2)], core_recv.at[0])
    for i in range(2):
        deep[other + i] = acc[4 * core + other + i] + half[other + i]
    sibling = at(y, 2 * gray(2 * bit1 + 1 - bit0) + parity, core)
    to_sibling = remote(deep.at[pl.ds(other, 2)], sib, sib_send, sib_recv, sibling)
    to_sibling.start()
    arrived(half.at[pl.ds(own, 2)], core_recv.at[1])
    for i in range(2):
        deep[own + i] = acc[4 * core + own + i] + half[own + i]
    for i in range(4):
        gain3[i] = gains_of(deep[i])
    spot3 = 2 * core + block % 2
    for i in range(4):
        row_to = 8 * node + 4 * (block // 2) + ZZ_ORDER[i]

        @pl.when(row_to != row)
        def _(i=i, row_to=row_to):
            remote(gain3.at[i], home3.at[spot3], g3_send.at[i], g3_recv.at[spot3], row_to).start()

        @pl.when(row_to == row)
        def _(i=i):
            pltpu.make_async_copy(gain3.at[i], home3.at[spot3], g3_recv.at[spot3]).start()

    for z_from in range(NZ):
        arrived(part_z.at[z_from], pz_recv.at[z_from])
    total_z = part_z[0]
    for z_from in range(1, NZ):
        total_z = total_z + part_z[z_from]
    mine_x[...] = total_z
    here = 2 * x + core
    for step in range(1, 2 * NX):
        remote(
            mine_x, part_x.at[here], px_send.at[step], px_recv.at[here],
            at(y, z, (core + step) % 2), (x + step // 2) % NX,
        ).start()
    pltpu.make_async_copy(mine_x, part_x.at[here], px_recv.at[here]).start()

    arrived(sib, sib_recv)
    places = (bit0, 3 - bit0)
    homes1 = []
    for i in range(2):
        mid[i] = deep[own + i] + sib[i]
        row_to = at(2 * parity + block // 2, 2 * places[i] + core, block % 2)
        homes1.append(row_to)

        @pl.when(row_to != row)
        def _(i=i, row_to=row_to):
            remote(mid.at[i], low.at[bit1], low_send.at[i], low_recv.at[bit1], row_to).start()

        @pl.when(row_to == row)
        def _(i=i):
            pltpu.make_async_copy(mid.at[i], low.at[bit1], low_recv.at[bit1]).start()

    homes2 = []
    spot2 = block % 2
    for i in range(2):
        gain2[i] = gains_of(mid[i])
        row_to = 16 * (node // 2) + 8 * (block // 2) + 2 * places[i] + core
        homes2.append(row_to)

        @pl.when(row_to != row)
        def _(i=i, row_to=row_to):
            remote(gain2.at[i], home2.at[spot2], g2_send.at[i], g2_recv.at[spot2], row_to).start()

        @pl.when(row_to == row)
        def _(i=i):
            pltpu.make_async_copy(gain2.at[i], home2.at[spot2], g2_recv.at[spot2]).start()

    for i in range(4):
        arrived(home3.at[i], g3_recv.at[i])
        three_ref[2 * i:2 * i + 1, :] = home3[i, :, 0:64]
        three_ref[2 * i + 1:2 * i + 2, :] = home3[i, :, 64:128]

    for i in range(2 * NX):
        arrived(part_x.at[i], px_recv.at[i])
    total_x = part_x[0]
    for i in range(1, 2 * NX):
        total_x = total_x + part_x[i]
    scores = -total_x[0:8] / jnp.sqrt(total_x[8:16] + penalty)
    child_out[0, 0] = scores[0:2]
    child_out[1, 0] = scores[2:4]
    child_out[2, 0] = jnp.where(z < NZ // 2, scores[4:6], scores[6:8])

    for i in range(2):
        arrived(low.at[i], low_recv.at[i])
    last = gains_of(low[0] + low[1])
    one_ref[0:1, :] = last[:, 0:64]
    one_ref[1:2, :] = last[:, 64:128]
    for i in range(2):
        arrived(home2.at[i], g2_recv.at[i])
        two_ref[2 * i:2 * i + 1, :] = home2[i, :, 0:64]
        two_ref[2 * i + 1:2 * i + 2, :] = home2[i, :, 64:128]

    for z_to in range(NZ):
        @pl.when(z_to != z)
        def _(z_to=z_to):
            arrived(sent.at[z_to], z_send.at[z_to])
    for step in range(1, NY):
        arrived(part.at[step], py_send.at[step])
        arrived(got_y.at[step], y_send.at[step])
    for turn in range(2):
        arrived(half.at[pl.ds(0, 2)], core_send.at[turn])
    for step in range(1, NZ):
        arrived(mine_z, pz_send.at[step])
    for step in range(1, 2 * NX):
        arrived(mine_x, px_send.at[step])
    to_sibling.wait_send()
    for i in range(4):
        @pl.when(8 * node + 4 * (block // 2) + ZZ_ORDER[i] != row)
        def _(i=i):
            arrived(gain3.at[i], g3_send.at[i])
    for i in range(2):
        @pl.when(homes1[i] != row)
        def _(i=i):
            arrived(mid.at[i], low_send.at[i])

        @pl.when(homes2[i] != row)
        def _(i=i):
            arrived(gain2.at[i], g2_send.at[i])


def on_device(gradients, hessians, bin_words, children, split_feature, split_bin):
    dma = pltpu.SemaphoreType.DMA
    vmem = pl.BlockSpec(memory_space=pltpu.VMEM)
    smem = pl.BlockSpec(memory_space=pltpu.SMEM)
    return pl.pallas_call(
        kernel,
        out_shape=(
            jax.ShapeDtypeStruct((2, BINS), F32),
            jax.ShapeDtypeStruct((4, BINS), F32),
            jax.ShapeDtypeStruct((8, BINS), F32),
            jax.ShapeDtypeStruct((3, 1, 2, OUT), F32),
        ),
        in_specs=[smem, smem, vmem, vmem, vmem, vmem],
        out_specs=(vmem,) * 4,
        scratch_shapes=[
            pltpu.VMEM((ROWS_ALL, ROW_DEV), BF16),
            pltpu.VMEM((NZ, ROWS_ALL, SLOTS), BF16),
            pltpu.VMEM((NZ, ROWS_ALL, SLOTS), BF16),
            pltpu.VMEM((NY, NZ, ROWS_DST, SLOTS), BF16),
            pltpu.VMEM((8, KEEP, 128), F32),
            pltpu.VMEM((4, KEEP, 128), F32),
            pltpu.VMEM((4, KEEP, 128), F32),
            pltpu.VMEM((2, KEEP, 128), F32),
            pltpu.VMEM((2, KEEP, 128), F32),
            pltpu.VMEM((2, KEEP, 128), F32),
            pltpu.VMEM((4, 1, 128), F32),
            pltpu.VMEM((4, 1, 128), F32),
            pltpu.VMEM((2, 1, 128), F32),
            pltpu.VMEM((2, 1, 128), F32),
            pltpu.VMEM((NY, 16, 128), F32),
            pltpu.VMEM((NY, 16, 128), F32),
            pltpu.VMEM((16, 128), F32),
            pltpu.VMEM((NZ, 16, 128), F32),
            pltpu.VMEM((16, 128), F32),
            pltpu.VMEM((2 * NX, 16, 128), F32),
            dma((NZ,)), dma((NZ,)), dma((NY,)), dma((NY,)), dma((2,)), dma((2,)), dma, dma,
            dma((2,)), dma((2,)), dma((4,)), dma((4,)), dma((2,)), dma((2,)),
            dma((NY,)), dma((NY,)), dma((NZ,)), dma((NZ,)), dma((2 * NX,)), dma((2 * NX,)),
        ],
        compiler_params=pltpu.CompilerParams(
            collective_id=0, has_side_effects=True, vmem_limit_bytes=32 << 20
        ),
    )(split_feature, split_bin, gradients, hessians.reshape(1, -1), bin_words, children)


def solution(mesh):
    placed = (P("rows", None), P("rows"), P("feat", "rows"), P(None, "rows"), P(), P())
    return jax.shard_map(
        on_device,
        mesh=mesh,
        in_specs=placed,
        out_specs=(
            P("rows", "feat"),
            P("rows", "feat"),
            P("rows", "feat"),
            P(None, "rows", None, None),
        ),
        check_vma=False,
    )
```

```python
import jax
import jax.numpy as jnp
from jax import lax
from jax.experimental import pallas as pl
from jax.experimental.pallas import tpu as pltpu
from jax.sharding import PartitionSpec as P

BINS = 64
OUT = 128
LEVELS = 3
SPLITS = 14
ROW_DEV = 512
SLOTS = 128
NY, NZ, NX = 4, 8, 4
HALF = OUT // 2
PIECE = HALF + 64
GOES_Y = HALF + 16
KEEP = OUT + 8
MESH = pl.DeviceIdType.MESH
F32 = jnp.float32
BF16 = jnp.bfloat16

penalty = 1.0
NEAR = (0, 1, 7, 2, 6, 3, 5, 4)


def block_of(y, upper):
    block = 2 * (((y + 1) // 2) % 2) + y // 2
    return block + upper * (3 - 2 * block)


def nt_dot(left, right):
    return lax.dot_general(left, right, (((1,), (1,)), ((), ())), preferred_element_type=F32)


def ones_where(condition):
    return condition.astype(F32).astype(BF16)


def gains_of(left):
    total = jnp.broadcast_to(left[:, 127:128], left.shape)
    right = total - left

    def term(part):
        square = part[:OUT] * part[:OUT]
        return jnp.sum(square, axis=0, keepdims=True) / (part[OUT:OUT + 1] + penalty)

    return (term(left) + term(right) - term(total)) / OUT


def kernel(
    split_feature_any, split_bin_any, grad_any, hess_any, word_any, child_any,
    one_ref, two_ref, three_ref, child_out,
    split_feature, split_bin, grad_ref, hess_ref, word_ref, child_ref,
    sent, sent_h, got_z, got_h, got_y, got_yh, got_x, codes_here,
    acc, half, deep, sib, mid, low,
    gain3, home3, gain2, home2, part, part_y, mine_z, part_z, mine_x, part_x,
    in_sem, z_send, z_recv, zh_send, zh_recv, y_send, y_recv, yh_send, yh_recv,
    relay_send, x_send, x_recv, core_send, core_recv, sib_send, sib_recv,
    low_send, low_recv, g3_send, g3_recv, g2_send, g2_recv,
    py_send, py_recv, pz_send, pz_recv, px_send, px_recv,
):
    row = lax.axis_index("rows")
    x = lax.axis_index("feat")
    core = row % 2
    z = (row // 2) % NZ
    y = row // 16
    upper = z // 4
    block = block_of(y, upper)
    kind = (z + upper) % 2
    own = 2 * kind
    other = 2 - own
    leaving = []

    def at(y_to, z_to, core_to):
        return y_to * 16 + z_to * 2 + core_to

    def remote(src, dst, send, recv, row_to, x_to=None):
        return pltpu.make_async_remote_copy(
            src_ref=src, dst_ref=dst, send_sem=send, recv_sem=recv,
            device_id=(row_to, x if x_to is None else x_to), device_id_type=MESH,
        )

    def arrived(ref, sem):
        pltpu.make_async_copy(ref, ref, sem).wait()

    def left_with(ref, sem):
        leaving.append(lambda: arrived(ref, sem))

    inputs = [
        pltpu.make_async_copy(src, dst, in_sem.at[i])
        for i, (src, dst) in enumerate((
            (child_any, child_ref), (hess_any, hess_ref), (word_any, word_ref),
            (grad_any, grad_ref), (split_feature_any, split_feature), (split_bin_any, split_bin),
        ))
    ]
    for copy in inputs:
        copy.start()

    barrier = pltpu.get_barrier_semaphore()

    def greet(row_to, x_to):
        pl.semaphore_signal(barrier, inc=1, device_id=(row_to, x_to), device_id_type=MESH)

    for step in (4, 3, 5, 2, 6, 1, 7):
        greet(at(y, (z + step) % NZ, core), x)
    for step in (2, 1, 3):
        greet(at((y + step) % NY, z, core), x)
    for step in range(1, 2 * NX):
        greet(at(y, z, (core + step) % 2), (x + step // 2) % NX)
    for copy in inputs:
        copy.wait()

    child = child_ref[...]
    node1 = child[0:1]
    node2 = node1 * 2 + child[1:2]
    node3 = node2 * 2 + child[2:3]
    at_node = (lax.broadcasted_iota(jnp.int32, (8, ROW_DEV), 0) == node3).astype(F32)
    upto = ones_where(
        lax.broadcasted_iota(jnp.int32, (ROW_DEV, ROW_DEV), 0)
        <= lax.broadcasted_iota(jnp.int32, (ROW_DEV, ROW_DEV), 1)
    )
    running = jnp.dot(at_node.astype(BF16), upto, preferred_element_type=F32)
    rank = jnp.sum(at_node * running, axis=0, keepdims=True).astype(jnp.int32) - 1
    slot = node3 * SLOTS + rank

    hess = hess_ref[...].reshape(1, ROW_DEV).astype(F32)
    outputs_all = grad_ref[...].astype(F32).T
    outputs_half = jnp.where(x % 2 == 0, outputs_all[:HALF], outputs_all[HALF:]).astype(BF16)
    words = word_ref[...]
    natural = jnp.concatenate(
        [jnp.bitwise_and(words, 63), jnp.bitwise_and(jnp.right_shift(words, 6), 63)], 0
    ).astype(F32).astype(BF16)
    spot64 = lax.broadcasted_iota(jnp.int32, (64, 1), 0)
    source64 = (
        32 * jnp.bitwise_and(jnp.right_shift(spot64, 3), 1)
        + 16 * jnp.right_shift(spot64, 5)
        + 2 * jnp.bitwise_and(spot64, 7)
        + jnp.bitwise_and(jnp.right_shift(spot64, 4), 1)
    )
    moved = ones_where(lax.broadcasted_iota(jnp.int32, (64, 64), 1) == source64)
    code_rows = jnp.dot(moved, natural, preferred_element_type=F32).astype(BF16)
    hess_tile = jnp.concatenate([hess, jnp.zeros((15, ROW_DEV), F32)], 0).astype(BF16)
    packed = jnp.concatenate([outputs_half, code_rows, hess_tile], 0)
    for pair in range(NZ // 2):
        wanted = lax.broadcasted_iota(jnp.int32, (2 * SLOTS, ROW_DEV), 0) + pair * 2 * SLOTS
        chosen = nt_dot(packed, ones_where(wanted == slot))
        for side in range(2):
            lanes = slice(side * SLOTS, (side + 1) * SLOTS)
            sent[2 * pair + side] = chosen[:PIECE, lanes].astype(BF16)
            sent_h[2 * pair + side] = chosen[PIECE:PIECE + 1, lanes]
    got_h[0] = sent_h[z]

    pl.semaphore_wait(barrier, (NZ - 1) + (NY - 1) + (2 * NX - 1))
    for step in (1, 7, 2, 6, 3, 5, 4):
        z_to = (z + step) % NZ
        place = NEAR.index((NZ - step) % NZ)
        remote(
            sent.at[z_to], got_z.at[place - 1], z_send.at[step], z_recv.at[place], at(y, z_to, core)
        ).start()
        left_with(sent.at[step], z_send.at[step])
    for step in (1, 7, 2, 6, 3, 5, 4):
        z_to = (z + step) % NZ
        place = NEAR.index((NZ - step) % NZ)
        remote(
            sent_h.at[z_to], got_h.at[place], zh_send, zh_recv, at(y, z_to, core)
        ).start()
    left_with(got_h.at[pl.ds(1, NZ - 1)], zh_send)

    rows32 = lax.broadcasted_iota(jnp.int32, (32, 1), 0)
    yy = jnp.right_shift(rows32, 3)
    which = jnp.bitwise_and(jnp.right_shift(rows32, 1), 3)
    right_side = jnp.bitwise_and(rows32, 1)
    is_one, is_two = which == 0, which == 1
    node_row = jnp.where(
        is_one, jnp.right_shift(yy, 1), jnp.where(is_two, yy, 2 * yy + which - 2)
    )
    split_row = node_row + jnp.where(is_one, 0, jnp.where(is_two, 2, 6))
    feature_row = jnp.zeros((32, 1), jnp.int32)
    bin_row = jnp.zeros((32, 1), jnp.int32)
    for s in range(SPLITS):
        feature_row = jnp.where(split_row == s, split_feature[s], feature_row)
        bin_row = jnp.where(split_row == s, split_bin[s], bin_row)
    inner = jnp.bitwise_and(feature_row, 63)
    place = (
        32 * jnp.right_shift(inner, 5)
        + 16 * jnp.bitwise_and(jnp.right_shift(inner, 1), 1)
        + 8 * jnp.bitwise_and(inner, 1)
        + jnp.bitwise_and(jnp.right_shift(inner, 2), 7)
    )
    panel_row = jnp.right_shift(feature_row, 6)
    spot = ones_where(lax.broadcasted_iota(jnp.int32, (32, 64), 1) == place)
    code_row = jnp.dot(spot, code_rows, preferred_element_type=F32).astype(jnp.int32)
    node_here = jnp.where(is_one, node1, jnp.where(is_two, node2, node3))
    goes_right = (code_row > bin_row).astype(jnp.int32)
    wanted_row = (node_here == node_row) & (panel_row == x) & (goes_right == right_side)
    wanted_row = wanted_row.astype(F32)
    sums = jnp.dot(wanted_row.astype(BF16), grad_ref[...], preferred_element_type=F32)
    sums_h = jnp.sum(wanted_row * hess, axis=1, keepdims=True)
    for y_to in range(NY):
        part[y_to, 0:8] = sums[8 * y_to:8 * y_to + 8]
        part[y_to, 8:16] = jnp.broadcast_to(sums_h[8 * y_to:8 * y_to + 8], (8, OUT))
    for step in range(1, NY):
        y_to = (y + step) % NY
        remote(
            part.at[y_to], part_y.at[y], py_send.at[step], py_recv.at[y], at(y_to, z, core)
        ).start()
        left_with(part.at[step], py_send.at[step])
    pltpu.make_async_copy(part.at[y], part_y.at[y], py_recv.at[y]).start()

    def piece(place):
        return sent.at[z] if place == 0 else got_z.at[place - 1]

    def to_x(src, offset, place):
        step = 1 - 2 * (place % 2)
        remote(
            src, got_x.at[offset, place], x_send.at[place % 2], x_recv.at[offset],
            row, (x + step) % NX,
        ).start()

    def from_z(group):
        for place in (2 * group, 2 * group + 1):
            if place:
                arrived(got_z.at[place - 1], z_recv.at[place])
            here = piece(place)
            for step in (1, 3):
                remote(
                    here.at[pl.ds(0, HALF)], got_y.at[NY - step - 1, place, pl.ds(0, HALF)],
                    y_send.at[step], y_recv.at[NY - step - 1, group], at((y + step) % NY, z, core),
                ).start()
            for step in (1, 3, 2):
                y_to = (y + step) % NY
                start = pl.multiple_of(HALF + 16 * block_of(y_to, upper), 16)
                remote(
                    here.at[pl.ds(start, 16)], got_y.at[NY - step - 1, place, pl.ds(HALF, 16)],
                    y_send.at[step], y_recv.at[NY - step - 1, group], at(y_to, z, core),
                ).start()
            to_x(here.at[pl.ds(0, HALF)], 0, place)

    def from_y(offset, group):
        arrived(got_y.at[offset - 1, pl.ds(2 * group, 2)], y_recv.at[offset - 1, group])
        if (offset, group % 2) in ((3, 0), (1, 1)):
            step = 1 if offset == 3 else 3
            places = pl.ds(2 * group, 2)
            remote(
                got_y.at[offset - 1, places, pl.ds(0, HALF)], got_y.at[1, places, pl.ds(0, HALF)],
                relay_send.at[group], y_recv.at[1, group], at((y + step) % NY, z, core),
            ).start()
            left_with(got_y.at[0, pl.ds(0, 2), pl.ds(0, HALF)], relay_send.at[group])
        for place in (2 * group, 2 * group + 1):
            to_x(got_y.at[offset - 1, place, pl.ds(0, HALF)], offset, place)

    bins = lax.broadcasted_iota(jnp.int32, (BINS, 1), 0).astype(F32)

    def add_rows(offset, first=False, after=None):
        arrived(got_x.at[offset], x_recv.at[offset])
        if offset == 0:
            pieces = [piece(i) for i in range(NZ)]
            start = pl.multiple_of(HALF + 16 * block, 16)
            kept = [ref[0:HALF, :] for ref in pieces]
            codes = [ref[pl.ds(start, 16), :] for ref in pieces]
            weights = [got_h[i] for i in range(NZ)]
        else:
            arrived(got_yh.at[offset - 1], yh_recv.at[offset - 1])
            kept = [got_y[offset - 1, i, 0:HALF, :] for i in range(NZ)]
            codes = [got_y[offset - 1, i, HALF:GOES_Y, :] for i in range(NZ)]
            weights = [got_yh[offset - 1, i] for i in range(NZ)]
        tile = jnp.concatenate(
            [jnp.concatenate(weights, 1), jnp.zeros((15, NZ * SLOTS), F32)], 0
        ).astype(BF16)
        values = jnp.concatenate([
            jnp.concatenate(kept, 1),
            jnp.concatenate([got_x[offset, i] for i in range(NZ)], 1),
            tile,
        ], 0)
        codes_here[...] = jnp.concatenate(codes, 1).astype(F32)
        for turn, (core_to, base) in enumerate(
            ((1 - core, other), (1 - core, own), (core, other), (core, own))
        ):
            masks = []
            for i in range(2):
                high = (2 * (base + i) + 7 * core_to) % 8
                for line in (high, 8 + high):
                    masks.append(ones_where(codes_here[pl.ds(line, 1), :] <= bins))
            found = nt_dot(values, jnp.concatenate(masks, 0))
            for i in range(2):
                new = found[:KEEP, 128 * i:128 * i + 128]
                if first:
                    acc[4 * core_to + base + i] = new
                else:
                    acc[4 * core_to + base + i] += new
            if after is not None:
                after(turn)

    buddy = at(y, z, 1 - core)

    def to_buddy(turn):
        if turn < 2:
            base = (other, own)[turn]
            for i in range(2):
                remote(
                    acc.at[4 * (1 - core) + base + i], half.at[base + i],
                    core_send.at[2 * turn + i], core_recv.at[2 * turn + i], buddy,
                ).start()
                left_with(half.at[0], core_send.at[2 * turn + i])

    from_z(0)
    from_z(1)
    from_y(1, 0)
    from_y(3, 0)
    from_z(2)
    from_y(1, 1)
    from_y(3, 1)
    from_z(3)
    arrived(got_h.at[pl.ds(1, NZ - 1)], zh_recv)
    for step in range(1, NY):
        remote(
            got_h, got_yh.at[NY - step - 1], yh_send.at[step], yh_recv.at[NY - step - 1],
            at((y + step) % NY, z, core),
        ).start()
        left_with(got_h, yh_send.at[step])
    from_y(2, 0)
    from_y(1, 2)
    from_y(3, 2)
    from_y(2, 1)
    from_y(1, 3)
    from_y(3, 3)
    for step in (1, 3):
        left_with(got_y.at[0], y_send.at[step])
    left_with(got_y.at[0, pl.ds(0, NZ), pl.ds(0, 16)], y_send.at[2])
    for y_from in range(NY):
        arrived(part_y.at[y_from], py_recv.at[y_from])
    mine_z[...] = (part_y[0] + part_y[1]) + (part_y[2] + part_y[3])
    for step in range(1, NZ):
        remote(
            mine_z, part_z.at[z], pz_send.at[step], pz_recv.at[z], at(y, (z + step) % NZ, core)
        ).start()
        left_with(mine_z, pz_send.at[step])
    pltpu.make_async_copy(mine_z, part_z.at[z], pz_recv.at[z]).start()
    add_rows(0, first=True)
    from_y(2, 2)
    add_rows(1)
    from_y(2, 3)
    for side in range(2):
        left_with(got_x.at[pl.ds(0, 2)], x_send.at[side])
    add_rows(3)
    add_rows(2, after=to_buddy)

    sibling = at(y, z + 1 - 2 * (z % 2), core)
    for i in range(2):
        arrived(half.at[other + i], core_recv.at[i])
        deep[other + i] = acc[4 * core + other + i] + half[other + i]
        remote(deep.at[other + i], sib.at[i], sib_send.at[i], sib_recv.at[i], sibling).start()
        left_with(sib.at[i], sib_send.at[i])
    for i in range(2):
        arrived(half.at[own + i], core_recv.at[2 + i])
        deep[own + i] = acc[4 * core + own + i] + half[own + i]

    def hand_over(src, dst, send, recv, row_to):
        @pl.when(row_to != row)
        def _():
            remote(src, dst, send, recv, row_to).start()

        @pl.when(row_to == row)
        def _():
            pltpu.make_async_copy(src, dst, recv).start()

        def leave():
            @pl.when(row_to != row)
            def _():
                arrived(src, send)

        leaving.append(leave)

    spot3 = 2 * core + block % 2
    for i in range(4):
        gain3[i] = gains_of(deep[i])
    for i in range(4):
        row_to = 8 * z + 4 * (block // 2) + (i + 3 * core) % 4
        hand_over(gain3.at[i], home3.at[spot3], g3_send.at[i], g3_recv.at[spot3], row_to)

    for z_from in range(NZ):
        arrived(part_z.at[z_from], pz_recv.at[z_from])
    total_z = part_z[0]
    for z_from in range(1, NZ):
        total_z = total_z + part_z[z_from]
    mine_x[...] = total_z
    here = 2 * x + core
    for step in range(1, 2 * NX):
        remote(
            mine_x, part_x.at[here], px_send.at[step], px_recv.at[here],
            at(y, z, (core + step) % 2), (x + step // 2) % NX,
        ).start()
        left_with(mine_x, px_send.at[step])
    pltpu.make_async_copy(mine_x, part_x.at[here], px_recv.at[here]).start()

    high_bits = [(2 * (own + i) + 7 * core) % 8 for i in range(2)]
    which1 = (z // 2) % 2
    for i in range(2):
        arrived(sib.at[i], sib_recv.at[i])
        mid[i] = deep[own + i] + sib[i]
        hand_over(
            mid.at[i], low.at[which1], low_send.at[i], low_recv.at[which1],
            at(2 * upper + block // 2, high_bits[i], block % 2),
        )
    spot2 = block % 2
    for i in range(2):
        gain2[i] = gains_of(mid[i])
        hand_over(
            gain2.at[i], home2.at[spot2], g2_send.at[i], g2_recv.at[spot2],
            16 * (z // 2) + 8 * (block // 2) + high_bits[i],
        )

    for i in range(4):
        arrived(home3.at[i], g3_recv.at[i])
        three_ref[2 * i:2 * i + 1, :] = home3[i, :, 0:64]
        three_ref[2 * i + 1:2 * i + 2, :] = home3[i, :, 64:128]

    for i in range(2 * NX):
        arrived(part_x.at[i], px_recv.at[i])
    total_x = part_x[0]
    for i in range(1, 2 * NX):
        total_x = total_x + part_x[i]
    scores = -total_x[0:8] / jnp.sqrt(total_x[8:16] + penalty)
    child_out[0, 0] = scores[0:2]
    child_out[1, 0] = scores[2:4]
    child_out[2, 0] = jnp.where(z < NZ // 2, scores[4:6], scores[6:8])

    for i in range(2):
        arrived(low.at[i], low_recv.at[i])
    last = gains_of(low[0] + low[1])
    one_ref[0:1, :] = last[:, 0:64]
    one_ref[1:2, :] = last[:, 64:128]
    for i in range(2):
        arrived(home2.at[i], g2_recv.at[i])
        two_ref[2 * i:2 * i + 1, :] = home2[i, :, 0:64]
        two_ref[2 * i + 1:2 * i + 2, :] = home2[i, :, 64:128]

    for leave in leaving:
        leave()


def on_device(gradients, hessians, bin_words, children, split_feature, split_bin):
    dma = pltpu.SemaphoreType.DMA
    vmem = pl.BlockSpec(memory_space=pltpu.VMEM)
    return pl.pallas_call(
        kernel,
        out_shape=(
            jax.ShapeDtypeStruct((2, BINS), F32),
            jax.ShapeDtypeStruct((4, BINS), F32),
            jax.ShapeDtypeStruct((8, BINS), F32),
            jax.ShapeDtypeStruct((LEVELS, 1, 2, OUT), F32),
        ),
        in_specs=[pl.BlockSpec(memory_space=pl.ANY)] * 6,
        out_specs=(vmem,) * 4,
        scratch_shapes=[
            pltpu.SMEM((SPLITS,), jnp.int32),
            pltpu.SMEM((SPLITS,), jnp.int32),
            pltpu.VMEM((ROW_DEV, OUT), BF16),
            pltpu.VMEM((ROW_DEV,), BF16),
            pltpu.VMEM((32, ROW_DEV), jnp.int32),
            pltpu.VMEM((LEVELS, ROW_DEV), jnp.int32),
            pltpu.VMEM((NZ, PIECE, SLOTS), BF16),
            pltpu.VMEM((NZ, 1, SLOTS), F32),
            pltpu.VMEM((NZ - 1, PIECE, SLOTS), BF16),
            pltpu.VMEM((NZ, 1, SLOTS), F32),
            pltpu.VMEM((NY - 1, NZ, GOES_Y, SLOTS), BF16),
            pltpu.VMEM((NY - 1, NZ, 1, SLOTS), F32),
            pltpu.VMEM((NY, NZ, HALF, SLOTS), BF16),
            pltpu.VMEM((16, NZ * SLOTS), F32),
            pltpu.VMEM((8, KEEP, 128), F32),
            pltpu.VMEM((4, KEEP, 128), F32),
            pltpu.VMEM((4, KEEP, 128), F32),
            pltpu.VMEM((2, KEEP, 128), F32),
            pltpu.VMEM((2, KEEP, 128), F32),
            pltpu.VMEM((2, KEEP, 128), F32),
            pltpu.VMEM((4, 1, 128), F32),
            pltpu.VMEM((4, 1, 128), F32),
            pltpu.VMEM((2, 1, 128), F32),
            pltpu.VMEM((2, 1, 128), F32),
            pltpu.VMEM((NY, 16, 128), F32),
            pltpu.VMEM((NY, 16, 128), F32),
            pltpu.VMEM((16, 128), F32),
            pltpu.VMEM((NZ, 16, 128), F32),
            pltpu.VMEM((16, 128), F32),
            pltpu.VMEM((2 * NX, 16, 128), F32),
            dma((6,)), dma((NZ,)), dma((NZ,)), dma, dma, dma((NY,)), dma((NY - 1, 4)),
            dma((NY,)), dma((NY - 1,)), dma((4,)), dma((2,)), dma((NY,)),
            dma((4,)), dma((4,)), dma((2,)), dma((2,)),
            dma((2,)), dma((2,)), dma((4,)), dma((4,)), dma((2,)), dma((2,)),
            dma((NY,)), dma((NY,)), dma((NZ,)), dma((NZ,)), dma((2 * NX,)), dma((2 * NX,)),
        ],
        compiler_params=pltpu.CompilerParams(collective_id=0, has_side_effects=True),
    )(split_feature, split_bin, gradients, hessians, bin_words, children)


def solution(mesh):
    placed = (P("rows", None), P("rows"), P("feat", "rows"), P(None, "rows"), P(), P())
    return jax.shard_map(
        on_device,
        mesh=mesh,
        in_specs=placed,
        out_specs=(
            P("rows", "feat"),
            P("rows", "feat"),
            P("rows", "feat"),
            P(None, "rows", None, None),
        ),
        check_vma=False,
    )
```

```python
import jax
import jax.numpy as jnp
from jax import lax
from jax.experimental import pallas as pl
from jax.experimental.pallas import tpu as pltpu
from jax.sharding import PartitionSpec as P

BINS = 64
OUT = 128
LEVELS = 3
SPLITS = 14
ROW_DEV = 512
SLOTS = 128
NY, NZ, NX = 4, 8, 4
HALF = OUT // 2
PIECE = HALF + 64
GOES_Y = HALF + 16
KEEP = OUT + 8
MESH = pl.DeviceIdType.MESH
F32 = jnp.float32
BF16 = jnp.bfloat16

penalty = 1.0
DIRECT = (3,)
NEAR = (0, 1, 7, 2, 6, 3, 5, 4)


def block_of(y, upper):
    block = 2 * (((y + 1) // 2) % 2) + y // 2
    return block + upper * (3 - 2 * block)


def nt_dot(left, right):
    return lax.dot_general(left, right, (((1,), (1,)), ((), ())), preferred_element_type=F32)


def ones_where(condition):
    return condition.astype(F32).astype(BF16)


def gains_of(left):
    total = jnp.broadcast_to(left[:, 127:128], left.shape)
    right = total - left

    def term(part):
        square = part[:OUT] * part[:OUT]
        return jnp.sum(square, axis=0, keepdims=True) / (part[OUT:OUT + 1] + penalty)

    return (term(left) + term(right) - term(total)) / OUT


def kernel(
    split_feature_any, split_bin_any, grad_any, hess_any, word_any, child_any,
    out_ref,
    split_feature, split_bin, grad_ref, hess_ref, word_ref, child_ref,
    sent, sent_h, got_z, got_h, got_y, got_yh, got_x, codes_here,
    acc, half, deep, sib, mid, low,
    gain3, home3, gain2, home2, part, part_y, mine_z, part_z, mine_x, part_x,
    in_sem, z_send, z_recv, zh_send, zh_recv, y_send, y_recv, yh_send, yh_recv,
    relay_send, x_send, x_recv, core_send, core_recv, sib_send, sib_recv,
    low_send, low_recv, g3_send, g3_recv, g2_send, g2_recv,
    py_send, py_recv, pz_send, pz_recv, px_send, px_recv,
):
    row = lax.axis_index("rows")
    x = lax.axis_index("feat")
    core = row % 2
    z = (row // 2) % NZ
    y = row // 16
    upper = z // 4
    block = block_of(y, upper)
    kind = (z + upper) % 2
    own = 2 * kind
    other = 2 - own
    leaving = []

    def at(y_to, z_to, core_to):
        return y_to * 16 + z_to * 2 + core_to

    def remote(src, dst, send, recv, row_to, x_to=None):
        return pltpu.make_async_remote_copy(
            src_ref=src, dst_ref=dst, send_sem=send, recv_sem=recv,
            device_id=(row_to, x if x_to is None else x_to), device_id_type=MESH,
        )

    def arrived(ref, sem):
        pltpu.make_async_copy(ref, ref, sem).wait()

    def left_with(ref, sem):
        leaving.append(lambda: arrived(ref, sem))

    inputs = [
        pltpu.make_async_copy(src, dst, in_sem.at[i])
        for i, (src, dst) in enumerate((
            (child_any, child_ref), (hess_any, hess_ref), (word_any, word_ref),
            (grad_any, grad_ref), (split_feature_any, split_feature), (split_bin_any, split_bin),
        ))
    ]
    for copy in inputs:
        copy.start()

    barrier = pltpu.get_barrier_semaphore()

    def greet(row_to, x_to):
        pl.semaphore_signal(barrier, inc=1, device_id=(row_to, x_to), device_id_type=MESH)

    for step in (4, 3, 5, 2, 6, 1, 7):
        greet(at(y, (z + step) % NZ, core), x)
    for step in (2, 1, 3):
        greet(at((y + step) % NY, z, core), x)
    for step in range(1, 2 * NX):
        greet(at(y, z, (core + step) % 2), (x + step // 2) % NX)
    for copy in inputs:
        copy.wait()

    child = child_ref[...]
    node1 = child[0:1]
    node2 = node1 * 2 + child[1:2]
    node3 = node2 * 2 + child[2:3]
    at_node = (lax.broadcasted_iota(jnp.int32, (8, ROW_DEV), 0) == node3).astype(F32)
    upto = ones_where(
        lax.broadcasted_iota(jnp.int32, (ROW_DEV, ROW_DEV), 0)
        <= lax.broadcasted_iota(jnp.int32, (ROW_DEV, ROW_DEV), 1)
    )
    running = jnp.dot(at_node.astype(BF16), upto, preferred_element_type=F32)
    rank = jnp.sum(at_node * running, axis=0, keepdims=True).astype(jnp.int32) - 1
    slot = node3 * SLOTS + rank

    hess = hess_ref[...].reshape(1, ROW_DEV).astype(F32)
    outputs_all = grad_ref[...].astype(F32).T
    outputs_half = jnp.where(x % 2 == 0, outputs_all[:HALF], outputs_all[HALF:]).astype(BF16)
    words = word_ref[...]
    natural = jnp.concatenate(
        [jnp.bitwise_and(words, 63), jnp.bitwise_and(jnp.right_shift(words, 6), 63)], 0
    ).astype(F32).astype(BF16)
    spot64 = lax.broadcasted_iota(jnp.int32, (64, 1), 0)
    source64 = (
        32 * jnp.bitwise_and(jnp.right_shift(spot64, 3), 1)
        + 16 * jnp.right_shift(spot64, 5)
        + 2 * jnp.bitwise_and(spot64, 7)
        + jnp.bitwise_and(jnp.right_shift(spot64, 4), 1)
    )
    moved = ones_where(lax.broadcasted_iota(jnp.int32, (64, 64), 1) == source64)
    code_rows = jnp.dot(moved, natural, preferred_element_type=F32).astype(BF16)
    hess_tile = jnp.concatenate([hess, jnp.zeros((15, ROW_DEV), F32)], 0).astype(BF16)
    packed = jnp.concatenate([outputs_half, code_rows, hess_tile], 0)
    for pair in range(NZ // 2):
        wanted = lax.broadcasted_iota(jnp.int32, (2 * SLOTS, ROW_DEV), 0) + pair * 2 * SLOTS
        chosen = nt_dot(packed, ones_where(wanted == slot))
        for side in range(2):
            lanes = slice(side * SLOTS, (side + 1) * SLOTS)
            sent[2 * pair + side] = chosen[:PIECE, lanes].astype(BF16)
            sent_h[2 * pair + side] = chosen[PIECE:PIECE + 1, lanes]
    got_h[0] = sent_h[z]

    pl.semaphore_wait(barrier, (NZ - 1) + (NY - 1) + (2 * NX - 1))
    for step in (1, 7, 2, 6, 3, 5, 4):
        z_to = (z + step) % NZ
        place = NEAR.index((NZ - step) % NZ)
        remote(
            sent.at[z_to], got_z.at[place - 1], z_send.at[step], z_recv.at[place], at(y, z_to, core)
        ).start()
        left_with(sent.at[step], z_send.at[step])
    for step in (1, 7, 2, 6, 3, 5, 4):
        z_to = (z + step) % NZ
        place = NEAR.index((NZ - step) % NZ)
        remote(
            sent_h.at[z_to], got_h.at[place], zh_send, zh_recv, at(y, z_to, core)
        ).start()
    left_with(got_h.at[pl.ds(1, NZ - 1)], zh_send)

    rows32 = lax.broadcasted_iota(jnp.int32, (32, 1), 0)
    yy = jnp.right_shift(rows32, 3)
    which = jnp.bitwise_and(jnp.right_shift(rows32, 1), 3)
    right_side = jnp.bitwise_and(rows32, 1)
    is_one, is_two = which == 0, which == 1
    node_row = jnp.where(
        is_one, jnp.right_shift(yy, 1), jnp.where(is_two, yy, 2 * yy + which - 2)
    )
    split_row = node_row + jnp.where(is_one, 0, jnp.where(is_two, 2, 6))
    feature_row = jnp.zeros((32, 1), jnp.int32)
    bin_row = jnp.zeros((32, 1), jnp.int32)
    for s in range(SPLITS):
        feature_row = jnp.where(split_row == s, split_feature[s], feature_row)
        bin_row = jnp.where(split_row == s, split_bin[s], bin_row)
    inner = jnp.bitwise_and(feature_row, 63)
    place = (
        32 * jnp.right_shift(inner, 5)
        + 16 * jnp.bitwise_and(jnp.right_shift(inner, 1), 1)
        + 8 * jnp.bitwise_and(inner, 1)
        + jnp.bitwise_and(jnp.right_shift(inner, 2), 7)
    )
    panel_row = jnp.right_shift(feature_row, 6)
    spot = ones_where(lax.broadcasted_iota(jnp.int32, (32, 64), 1) == place)
    code_row = jnp.dot(spot, code_rows, preferred_element_type=F32).astype(jnp.int32)
    node_here = jnp.where(is_one, node1, jnp.where(is_two, node2, node3))
    goes_right = (code_row > bin_row).astype(jnp.int32)
    wanted_row = (node_here == node_row) & (panel_row == x) & (goes_right == right_side)
    wanted_row = wanted_row.astype(F32)
    sums = jnp.dot(wanted_row.astype(BF16), grad_ref[...], preferred_element_type=F32)
    sums_h = jnp.sum(wanted_row * hess, axis=1, keepdims=True)
    for y_to in range(NY):
        part[y_to, 0:8] = sums[8 * y_to:8 * y_to + 8]
        part[y_to, 8:16] = jnp.broadcast_to(sums_h[8 * y_to:8 * y_to + 8], (8, OUT))
    for step in range(1, NY):
        y_to = (y + step) % NY
        remote(
            part.at[y_to], part_y.at[y], py_send.at[step], py_recv.at[y], at(y_to, z, core)
        ).start()
        left_with(part.at[step], py_send.at[step])
    pltpu.make_async_copy(part.at[y], part_y.at[y], py_recv.at[y]).start()

    def piece(place):
        return sent.at[z] if place == 0 else got_z.at[place - 1]

    def to_x(src, offset, place):
        step = 1 - 2 * (place % 2)
        remote(
            src, got_x.at[offset, place], x_send.at[place % 2],
            x_recv.at[offset + 2 * int(offset == 2 and place >= NZ // 2)],
            row, (x + step) % NX,
        ).start()

    def from_z(group):
        for place in (2 * group, 2 * group + 1):
            if place:
                arrived(got_z.at[place - 1], z_recv.at[place])
            here = piece(place)
            for step in (1, 3, 2) if group in DIRECT else (1, 3):
                remote(
                    here.at[pl.ds(0, HALF)], got_y.at[NY - step - 1, place, pl.ds(0, HALF)],
                    y_send.at[step % 2 * step], y_recv.at[NY - step - 1, group],
                    at((y + step) % NY, z, core),
                ).start()
            for step in (1, 3, 2):
                y_to = (y + step) % NY
                start = pl.multiple_of(HALF + 16 * block_of(y_to, upper), 16)
                remote(
                    here.at[pl.ds(start, 16)], got_y.at[NY - step - 1, place, pl.ds(HALF, 16)],
                    y_send.at[step], y_recv.at[NY - step - 1, group], at(y_to, z, core),
                ).start()
            to_x(here.at[pl.ds(0, HALF)], 0, place)

    def from_y(offset, group):
        arrived(got_y.at[offset - 1, pl.ds(2 * group, 2)], y_recv.at[offset - 1, group])
        if group not in DIRECT and (offset, group % 2) in ((3, 0), (1, 1)):
            step = 1 if offset == 3 else 3
            places = pl.ds(2 * group, 2)
            remote(
                got_y.at[offset - 1, places, pl.ds(0, HALF)], got_y.at[1, places, pl.ds(0, HALF)],
                relay_send.at[group], y_recv.at[1, group], at((y + step) % NY, z, core),
            ).start()
            left_with(got_y.at[0, pl.ds(0, 2), pl.ds(0, HALF)], relay_send.at[group])
        for place in (2 * group, 2 * group + 1):
            to_x(got_y.at[offset - 1, place, pl.ds(0, HALF)], offset, place)

    bins = lax.broadcasted_iota(jnp.int32, (BINS, 1), 0).astype(F32)

    def add_rows(offset, first=False, after=None, places=range(NZ)):
        here_x = pl.ds(places[0], len(places))
        late = int(offset == 2 and places[0] > 0)
        arrived(got_x.at[offset, here_x], x_recv.at[offset + 2 * late])
        if offset == 0:
            pieces = [piece(i) for i in places]
            start = pl.multiple_of(HALF + 16 * block, 16)
            kept = [ref[0:HALF, :] for ref in pieces]
            codes = [ref[pl.ds(start, 16), :] for ref in pieces]
            weights = [got_h[i] for i in places]
        else:
            if not late:
                arrived(got_yh.at[offset - 1], yh_recv.at[offset - 1])
            kept = [got_y[offset - 1, i, 0:HALF, :] for i in places]
            codes = [got_y[offset - 1, i, HALF:GOES_Y, :] for i in places]
            weights = [got_yh[offset - 1, i] for i in places]
        tile = jnp.concatenate(
            [jnp.concatenate(weights, 1), jnp.zeros((15, len(places) * SLOTS), F32)], 0
        ).astype(BF16)
        values = jnp.concatenate([
            jnp.concatenate(kept, 1),
            jnp.concatenate([got_x[offset, i] for i in places], 1),
            tile,
        ], 0)
        codes_here[:, 0:len(places) * SLOTS] = jnp.concatenate(codes, 1).astype(F32)
        for turn, (core_to, base) in enumerate(
            ((1 - core, other), (1 - core, own), (core, other), (core, own))
        ):
            masks = []
            for i in range(2):
                high = (2 * (base + i) + 5 * core_to) % 8
                for line in (high, 8 + high):
                    masks.append(ones_where(codes_here[pl.ds(line, 1), 0:len(places) * SLOTS] <= bins))
            found = nt_dot(values, jnp.concatenate(masks, 0))
            for i in range(2):
                new = found[:KEEP, 128 * i:128 * i + 128]
                if first:
                    acc[4 * core_to + base + i] = new
                else:
                    acc[4 * core_to + base + i] += new
            if after is not None:
                after(turn)

    buddy = at(y, z, 1 - core)

    def to_buddy(turn):
        if turn < 2:
            base = (other, own)[turn]
            for i in range(2):
                remote(
                    acc.at[4 * (1 - core) + base + i], half.at[base + i],
                    core_send.at[2 * turn + i], core_recv.at[2 * turn + i], buddy,
                ).start()
                left_with(half.at[0], core_send.at[2 * turn + i])

    from_z(0)
    from_z(1)
    from_z(2)
    from_y(1, 0)
    from_y(3, 0)
    from_y(1, 1)
    from_y(3, 1)
    from_z(3)
    from_y(2, 0)
    from_y(1, 2)
    from_y(3, 2)
    from_y(2, 1)
    from_y(1, 3)
    from_y(3, 3)
    arrived(got_h.at[pl.ds(1, NZ - 1)], zh_recv)
    for step in range(1, NY):
        remote(
            got_h, got_yh.at[NY - step - 1], yh_send.at[step], yh_recv.at[NY - step - 1],
            at((y + step) % NY, z, core),
        ).start()
        left_with(got_h, yh_send.at[step])
    from_y(2, 2)
    from_y(2, 3)
    for y_from in range(NY):
        arrived(part_y.at[y_from], py_recv.at[y_from])
    mine_z[...] = (part_y[0] + part_y[1]) + (part_y[2] + part_y[3])
    for step in range(1, NZ):
        remote(
            mine_z, part_z.at[z], pz_send.at[step], pz_recv.at[z], at(y, (z + step) % NZ, core)
        ).start()
        left_with(mine_z, pz_send.at[step])
    pltpu.make_async_copy(mine_z, part_z.at[z], pz_recv.at[z]).start()
    for step in (1, 3):
        left_with(got_y.at[0], y_send.at[step])
    left_with(got_y.at[0, pl.ds(0, NZ), pl.ds(0, 16)], y_send.at[2])
    left_with(got_y.at[0, pl.ds(0, 2 * len(DIRECT)), pl.ds(0, HALF)], y_send.at[0])
    add_rows(0, first=True)
    add_rows(1)
    for side in range(2):
        left_with(got_x.at[pl.ds(0, 2)], x_send.at[side])
    add_rows(3)
    add_rows(2, places=range(NZ // 2))
    add_rows(2, after=to_buddy, places=range(NZ // 2, NZ))

    sibling = at(y, z + 1 - 2 * (z % 2), core)
    for i in range(2):
        arrived(half.at[other + i], core_recv.at[i])
        deep[other + i] = acc[4 * core + other + i] + half[other + i]
        remote(deep.at[other + i], sib.at[i], sib_send.at[i], sib_recv.at[i], sibling).start()
        left_with(sib.at[i], sib_send.at[i])
    for i in range(2):
        arrived(half.at[own + i], core_recv.at[2 + i])
        deep[own + i] = acc[4 * core + own + i] + half[own + i]

    def hand_over(src, dst, send, recv, row_to):
        @pl.when(row_to != row)
        def _():
            remote(src, dst, send, recv, row_to).start()

        @pl.when(row_to == row)
        def _():
            pltpu.make_async_copy(src, dst, recv).start()

        def leave():
            @pl.when(row_to != row)
            def _():
                arrived(src, send)

        leaving.append(leave)

    spot3 = 2 * core + block % 2
    for i in range(4):
        gain3[i] = gains_of(deep[i])
    for i in range(4):
        row_to = 8 * z + 4 * (block // 2) + (i + 2 * core) % 4
        hand_over(gain3.at[i], home3.at[spot3], g3_send.at[i], g3_recv.at[spot3], row_to)

    for z_from in range(NZ):
        arrived(part_z.at[z_from], pz_recv.at[z_from])
    total_z = part_z[0]
    for z_from in range(1, NZ):
        total_z = total_z + part_z[z_from]
    mine_x[...] = total_z
    here = 2 * x + core
    for step in range(1, 2 * NX):
        remote(
            mine_x, part_x.at[here], px_send.at[step], px_recv.at[here],
            at(y, z, (core + step) % 2), (x + step // 2) % NX,
        ).start()
        left_with(mine_x, px_send.at[step])
    pltpu.make_async_copy(mine_x, part_x.at[here], px_recv.at[here]).start()

    high_bits = [(2 * (own + i) + 5 * core) % 8 for i in range(2)]
    which1 = (z // 2) % 2
    for i in range(2):
        arrived(sib.at[i], sib_recv.at[i])
        mid[i] = deep[own + i] + sib[i]
        hand_over(
            mid.at[i], low.at[which1], low_send.at[i], low_recv.at[which1],
            at(2 * upper + block // 2, high_bits[i], block % 2),
        )
    spot2 = block % 2
    for i in range(2):
        gain2[i] = gains_of(mid[i])
        hand_over(
            gain2.at[i], home2.at[spot2], g2_send.at[i], g2_recv.at[spot2],
            16 * (z // 2) + 8 * (block // 2) + high_bits[i],
        )

    for i in range(4):
        arrived(home3.at[i], g3_recv.at[i])
        out_ref[i:i + 1, :] = home3[i]

    for i in range(2 * NX):
        arrived(part_x.at[i], px_recv.at[i])
    total_x = part_x[0]
    for i in range(1, 2 * NX):
        total_x = total_x + part_x[i]
    scores = -total_x[0:8] / jnp.sqrt(total_x[8:16] + penalty)
    out_ref[8:12, :] = scores[0:4]
    out_ref[12:14, :] = jnp.where(z < NZ // 2, scores[4:6], scores[6:8])

    for i in range(2):
        arrived(low.at[i], low_recv.at[i])
    last = gains_of(low[0] + low[1])
    out_ref[6:7, :] = last
    for i in range(2):
        arrived(home2.at[i], g2_recv.at[i])
        out_ref[4 + i:5 + i, :] = home2[i]

    for leave in leaving:
        leave()


def spread(all_ref, one_ref, two_ref, three_ref, child_out):
    for first, ref in ((0, three_ref), (4, two_ref), (6, one_ref)):
        for i in range(ref.shape[0] // 2):
            ref[2 * i:2 * i + 1, :] = all_ref[first + i:first + i + 1, 0:BINS]
            ref[2 * i + 1:2 * i + 2, :] = all_ref[first + i:first + i + 1, BINS:2 * BINS]
    for level in range(LEVELS):
        child_out[level, 0] = all_ref[8 + 2 * level:10 + 2 * level, :]


def on_device(gradients, hessians, bin_words, children, split_feature, split_bin):
    dma = pltpu.SemaphoreType.DMA
    vmem = pl.BlockSpec(memory_space=pltpu.VMEM)
    together = pl.pallas_call(
        kernel,
        out_shape=jax.ShapeDtypeStruct((16, 128), F32),
        in_specs=[pl.BlockSpec(memory_space=pl.ANY)] * 6,
        out_specs=vmem,
        scratch_shapes=[
            pltpu.SMEM((SPLITS,), jnp.int32),
            pltpu.SMEM((SPLITS,), jnp.int32),
            pltpu.VMEM((ROW_DEV, OUT), BF16),
            pltpu.VMEM((ROW_DEV,), BF16),
            pltpu.VMEM((32, ROW_DEV), jnp.int32),
            pltpu.VMEM((LEVELS, ROW_DEV), jnp.int32),
            pltpu.VMEM((NZ, PIECE, SLOTS), BF16),
            pltpu.VMEM((NZ, 1, SLOTS), F32),
            pltpu.VMEM((NZ - 1, PIECE, SLOTS), BF16),
            pltpu.VMEM((NZ, 1, SLOTS), F32),
            pltpu.VMEM((NY - 1, NZ, GOES_Y, SLOTS), BF16),
            pltpu.VMEM((NY - 1, NZ, 1, SLOTS), F32),
            pltpu.VMEM((NY, NZ, HALF, SLOTS), BF16),
            pltpu.VMEM((16, NZ * SLOTS), F32),
            pltpu.VMEM((8, KEEP, 128), F32),
            pltpu.VMEM((4, KEEP, 128), F32),
            pltpu.VMEM((4, KEEP, 128), F32),
            pltpu.VMEM((2, KEEP, 128), F32),
            pltpu.VMEM((2, KEEP, 128), F32),
            pltpu.VMEM((2, KEEP, 128), F32),
            pltpu.VMEM((4, 1, 128), F32),
            pltpu.VMEM((4, 1, 128), F32),
            pltpu.VMEM((2, 1, 128), F32),
            pltpu.VMEM((2, 1, 128), F32),
            pltpu.VMEM((NY, 16, 128), F32),
            pltpu.VMEM((NY, 16, 128), F32),
            pltpu.VMEM((16, 128), F32),
            pltpu.VMEM((NZ, 16, 128), F32),
            pltpu.VMEM((16, 128), F32),
            pltpu.VMEM((2 * NX, 16, 128), F32),
            dma((6,)), dma((NZ,)), dma((NZ,)), dma, dma, dma((NY,)), dma((NY - 1, 4)),
            dma((NY,)), dma((NY - 1,)), dma((4,)), dma((2,)), dma((NY + 1,)),
            dma((4,)), dma((4,)), dma((2,)), dma((2,)),
            dma((2,)), dma((2,)), dma((4,)), dma((4,)), dma((2,)), dma((2,)),
            dma((NY,)), dma((NY,)), dma((NZ,)), dma((NZ,)), dma((2 * NX,)), dma((2 * NX,)),
        ],
        compiler_params=pltpu.CompilerParams(collective_id=0, has_side_effects=True),
    )(split_feature, split_bin, gradients, hessians, bin_words, children)
    return pl.pallas_call(
        spread,
        out_shape=(
            jax.ShapeDtypeStruct((2, BINS), F32),
            jax.ShapeDtypeStruct((4, BINS), F32),
            jax.ShapeDtypeStruct((8, BINS), F32),
            jax.ShapeDtypeStruct((LEVELS, 1, 2, OUT), F32),
        ),
        in_specs=[vmem],
        out_specs=(vmem,) * 4,
    )(together)


def solution(mesh):
    placed = (P("rows", None), P("rows"), P("feat", "rows"), P(None, "rows"), P(), P())
    return jax.shard_map(
        on_device,
        mesh=mesh,
        in_specs=placed,
        out_specs=(
            P("rows", "feat"),
            P("rows", "feat"),
            P("rows", "feat"),
            P(None, "rows", None, None),
        ),
        check_vma=False,
    )
```

```python
import jax
import jax.numpy as jnp
from jax import lax
from jax.experimental import pallas as pl
from jax.experimental.pallas import tpu as pltpu
from jax.sharding import PartitionSpec as P

BINS = 64
OUT = 128
LEVELS = 3
SPLITS = 14
ROW_DEV = 512
SLOTS = 128
NY, NZ, NX = 4, 8, 4
HALF = OUT // 2
PIECE = HALF + 64
GOES_Y = HALF + 16
KEEP = OUT + 8
MESH = pl.DeviceIdType.MESH
F32 = jnp.float32
BF16 = jnp.bfloat16

penalty = 1.0
DIRECT = (0, 1, 2, 3)
NEAR = (0, 1, 7, 2, 6, 4, 3, 5)


def block_of(y, upper):
    block = 2 * (((y + 1) // 2) % 2) + y // 2
    return block + upper * (3 - 2 * block)


def nt_dot(left, right):
    return lax.dot_general(left, right, (((1,), (1,)), ((), ())), preferred_element_type=F32)


def ones_where(condition):
    return condition.astype(F32).astype(BF16)


def gains_of(left):
    total = jnp.broadcast_to(left[:, 127:128], left.shape)
    right = total - left

    def term(part):
        square = part[:OUT] * part[:OUT]
        return jnp.sum(square, axis=0, keepdims=True) / (part[OUT:OUT + 1] + penalty)

    return (term(left) + term(right) - term(total)) / OUT


def kernel(
    split_feature_any, split_bin_any, grad_any, hess_any, word_any, child_any,
    out_ref,
    split_feature, split_bin, grad_ref, hess_ref, word_ref, child_ref,
    sent, sent_h, got_z, got_h, got_y, got_yh, got_x, codes_here,
    acc, half, deep, sib, mid, low,
    gain3, home3, gain2, home2, part, part_y, mine_z, part_z, mine_x, part_x,
    in_sem, z_send, z_recv, zh_send, zh_recv, y_send, y_recv, yh_send, yh_recv,
    x_send, x_recv, core_send, core_recv, sib_send, sib_recv,
    low_send, low_recv, g3_send, g3_recv, g2_send, g2_recv,
    py_send, py_recv, pz_send, pz_recv, px_send, px_recv,
):
    row = lax.axis_index("rows")
    x = lax.axis_index("feat")
    core = row % 2
    z = (row // 2) % NZ
    y = row // 16
    upper = z // 4
    block = block_of(y, upper)
    kind = (z + upper) % 2
    own = 2 * kind
    other = 2 - own
    leaving = []

    def at(y_to, z_to, core_to):
        return y_to * 16 + z_to * 2 + core_to

    def remote(src, dst, send, recv, row_to, x_to=None):
        return pltpu.make_async_remote_copy(
            src_ref=src, dst_ref=dst, send_sem=send, recv_sem=recv,
            device_id=(row_to, x if x_to is None else x_to), device_id_type=MESH,
        )

    def arrived(ref, sem):
        pltpu.make_async_copy(ref, ref, sem).wait()

    def left_with(ref, sem):
        leaving.append(lambda: arrived(ref, sem))

    inputs = [
        pltpu.make_async_copy(src, dst, in_sem.at[i])
        for i, (src, dst) in enumerate((
            (child_any, child_ref), (hess_any, hess_ref), (word_any, word_ref),
            (grad_any, grad_ref), (split_feature_any, split_feature), (split_bin_any, split_bin),
        ))
    ]
    for copy in inputs:
        copy.start()

    barrier = pltpu.get_barrier_semaphore()

    def greet(row_to, x_to):
        pl.semaphore_signal(barrier, inc=1, device_id=(row_to, x_to), device_id_type=MESH)

    for step in (4, 3, 5, 2, 6, 1, 7):
        greet(at(y, (z + step) % NZ, core), x)
    for step in (2, 1, 3):
        greet(at((y + step) % NY, z, core), x)
    for step in (2, 1, 3):
        for side in (1, NX - 1):
            greet(at((y + step) % NY, z, core), (x + side) % NX)
    for step in range(1, 2 * NX):
        greet(at(y, z, (core + step) % 2), (x + step // 2) % NX)
    for copy in inputs:
        copy.wait()

    child = child_ref[...]
    node1 = child[0:1]
    node2 = node1 * 2 + child[1:2]
    node3 = node2 * 2 + child[2:3]
    at_node = (lax.broadcasted_iota(jnp.int32, (8, ROW_DEV), 0) == node3).astype(F32)
    upto = ones_where(
        lax.broadcasted_iota(jnp.int32, (ROW_DEV, ROW_DEV), 0)
        <= lax.broadcasted_iota(jnp.int32, (ROW_DEV, ROW_DEV), 1)
    )
    running = jnp.dot(at_node.astype(BF16), upto, preferred_element_type=F32)
    rank = jnp.sum(at_node * running, axis=0, keepdims=True).astype(jnp.int32) - 1
    slot = node3 * SLOTS + rank

    hess = hess_ref[...].reshape(1, ROW_DEV).astype(F32)
    outputs_all = grad_ref[...].astype(F32).T
    outputs_half = jnp.where(x % 2 == 0, outputs_all[:HALF], outputs_all[HALF:]).astype(BF16)
    words = word_ref[...]
    natural = jnp.concatenate(
        [jnp.bitwise_and(words, 63), jnp.bitwise_and(jnp.right_shift(words, 6), 63)], 0
    ).astype(F32).astype(BF16)
    spot64 = lax.broadcasted_iota(jnp.int32, (64, 1), 0)
    source64 = (
        32 * jnp.bitwise_and(jnp.right_shift(spot64, 3), 1)
        + 16 * jnp.right_shift(spot64, 5)
        + 2 * jnp.bitwise_and(spot64, 7)
        + jnp.bitwise_and(jnp.right_shift(spot64, 4), 1)
    )
    moved = ones_where(lax.broadcasted_iota(jnp.int32, (64, 64), 1) == source64)
    code_rows = jnp.dot(moved, natural, preferred_element_type=F32).astype(BF16)
    hess_tile = jnp.concatenate([hess, jnp.zeros((15, ROW_DEV), F32)], 0).astype(BF16)
    packed = jnp.concatenate([outputs_half, code_rows, hess_tile], 0)
    for pair in range(NZ // 2):
        wanted = lax.broadcasted_iota(jnp.int32, (2 * SLOTS, ROW_DEV), 0) + pair * 2 * SLOTS
        chosen = nt_dot(packed, ones_where(wanted == slot))
        for side in range(2):
            lanes = slice(side * SLOTS, (side + 1) * SLOTS)
            sent[2 * pair + side] = chosen[:PIECE, lanes].astype(BF16)
            sent_h[2 * pair + side] = chosen[PIECE:PIECE + 1, lanes]
    got_h[0] = sent_h[z]

    pl.semaphore_wait(barrier, (NZ - 1) + 3 * (NY - 1) + (2 * NX - 1))
    for step in (1, 7, 4, 2, 6, 3, 5):
        z_to = (z + step) % NZ
        place = NEAR.index((NZ - step) % NZ)
        remote(
            sent.at[z_to], got_z.at[place - 1], z_send.at[step], z_recv.at[place], at(y, z_to, core)
        ).start()
        left_with(sent.at[step], z_send.at[step])
    for step in (1, 7, 4, 2, 6, 3, 5):
        z_to = (z + step) % NZ
        place = NEAR.index((NZ - step) % NZ)
        remote(
            sent_h.at[z_to], got_h.at[place], zh_send, zh_recv, at(y, z_to, core)
        ).start()
    left_with(got_h.at[pl.ds(1, NZ - 1)], zh_send)

    rows32 = lax.broadcasted_iota(jnp.int32, (32, 1), 0)
    yy = jnp.right_shift(rows32, 3)
    which = jnp.bitwise_and(jnp.right_shift(rows32, 1), 3)
    right_side = jnp.bitwise_and(rows32, 1)
    is_one, is_two = which == 0, which == 1
    node_row = jnp.where(
        is_one, jnp.right_shift(yy, 1), jnp.where(is_two, yy, 2 * yy + which - 2)
    )
    split_row = node_row + jnp.where(is_one, 0, jnp.where(is_two, 2, 6))
    feature_row = jnp.zeros((32, 1), jnp.int32)
    bin_row = jnp.zeros((32, 1), jnp.int32)
    for s in range(SPLITS):
        feature_row = jnp.where(split_row == s, split_feature[s], feature_row)
        bin_row = jnp.where(split_row == s, split_bin[s], bin_row)
    inner = jnp.bitwise_and(feature_row, 63)
    place = (
        32 * jnp.right_shift(inner, 5)
        + 16 * jnp.bitwise_and(jnp.right_shift(inner, 1), 1)
        + 8 * jnp.bitwise_and(inner, 1)
        + jnp.bitwise_and(jnp.right_shift(inner, 2), 7)
    )
    panel_row = jnp.right_shift(feature_row, 6)
    spot = ones_where(lax.broadcasted_iota(jnp.int32, (32, 64), 1) == place)
    code_row = jnp.dot(spot, code_rows, preferred_element_type=F32).astype(jnp.int32)
    node_here = jnp.where(is_one, node1, jnp.where(is_two, node2, node3))
    goes_right = (code_row > bin_row).astype(jnp.int32)
    wanted_row = (node_here == node_row) & (panel_row == x) & (goes_right == right_side)
    wanted_row = wanted_row.astype(F32)
    sums = jnp.dot(wanted_row.astype(BF16), grad_ref[...], preferred_element_type=F32)
    sums_h = jnp.sum(wanted_row * hess, axis=1, keepdims=True)
    for y_to in range(NY):
        part[y_to, 0:8] = sums[8 * y_to:8 * y_to + 8]
        part[y_to, 8:16] = jnp.broadcast_to(sums_h[8 * y_to:8 * y_to + 8], (8, OUT))
    for step in range(1, NY):
        y_to = (y + step) % NY
        remote(
            part.at[y_to], part_y.at[y], py_send.at[step], py_recv.at[y], at(y_to, z, core)
        ).start()
        left_with(part.at[step], py_send.at[step])
    pltpu.make_async_copy(part.at[y], part_y.at[y], py_recv.at[y]).start()

    def piece(place):
        return sent.at[z] if place == 0 else got_z.at[place - 1]

    def to_x(src, offset, place, y_step=0):
        step = 1 - 2 * (place % 2)
        late = int(place >= NZ // 2)
        remote(
            src, got_x.at[offset, place], x_send.at[place % 2], x_recv.at[offset, late],
            at((y + y_step) % NY, z, core), (x + step) % NX,
        ).start()

    def from_z(group):
        for place in (2 * group, 2 * group + 1):
            if place:
                arrived(got_z.at[place - 1], z_recv.at[place])
            here = piece(place)
            for step in (1, 3, 2):
                remote(
                    here.at[pl.ds(0, HALF)], got_y.at[NY - step - 1, place, pl.ds(0, HALF)],
                    y_send.at[step], y_recv.at[NY - step - 1, group],
                    at((y + step) % NY, z, core),
                ).start()
            for step in (1, 3, 2):
                y_to = (y + step) % NY
                start = pl.multiple_of(HALF + 16 * block_of(y_to, upper), 16)
                remote(
                    here.at[pl.ds(start, 16)], got_y.at[NY - step - 1, place, pl.ds(HALF, 16)],
                    y_send.at[step], y_recv.at[NY - step - 1, group], at(y_to, z, core),
                ).start()
            for step in (0, 1, 3, 2) if group in DIRECT else (0,):
                to_x(here.at[pl.ds(0, HALF)], (NY - step) % NY, place, step)

    def from_y(offset, group):
        arrived(got_y.at[offset - 1, pl.ds(2 * group, 2)], y_recv.at[offset - 1, group])
        for place in (2 * group, 2 * group + 1) if group not in DIRECT else ():
            to_x(got_y.at[offset - 1, place, pl.ds(0, HALF)], offset, place)

    bins = lax.broadcasted_iota(jnp.int32, (BINS, 1), 0).astype(F32)

    def add_rows(offset, first=False, after=None, places=range(NZ)):
        here_x = pl.ds(places[0], len(places))
        late = int(places[0] > 0)
        arrived(got_x.at[offset, here_x], x_recv.at[offset, late])
        if offset == 0:
            pieces = [piece(i) for i in places]
            start = pl.multiple_of(HALF + 16 * block, 16)
            kept = [ref[0:HALF, :] for ref in pieces]
            codes = [ref[pl.ds(start, 16), :] for ref in pieces]
            weights = [got_h[i] for i in places]
        else:
            if not late:
                arrived(got_yh.at[offset - 1], yh_recv.at[offset - 1])
            kept = [got_y[offset - 1, i, 0:HALF, :] for i in places]
            codes = [got_y[offset - 1, i, HALF:GOES_Y, :] for i in places]
            weights = [got_yh[offset - 1, i] for i in places]
        tile = jnp.concatenate(
            [jnp.concatenate(weights, 1), jnp.zeros((15, len(places) * SLOTS), F32)], 0
        ).astype(BF16)
        values = jnp.concatenate([
            jnp.concatenate(kept, 1),
            jnp.concatenate([got_x[offset, i] for i in places], 1),
            tile,
        ], 0)
        codes_here[:, 0:len(places) * SLOTS] = jnp.concatenate(codes, 1).astype(F32)
        for turn, (core_to, base) in enumerate(
            ((1 - core, other), (1 - core, own), (core, other), (core, own))
        ):
            masks = []
            for i in range(2):
                high = (2 * (base + i) + 5 * core_to) % 8
                for line in (high, 8 + high):
                    masks.append(ones_where(codes_here[pl.ds(line, 1), 0:len(places) * SLOTS] <= bins))
            found = nt_dot(values, jnp.concatenate(masks, 0))
            for i in range(2):
                new = found[:KEEP, 128 * i:128 * i + 128]
                if first:
                    acc[4 * core_to + base + i] = new
                else:
                    acc[4 * core_to + base + i] += new
            if after is not None:
                after(turn)

    buddy = at(y, z, 1 - core)

    def to_buddy(turn):
        if turn < 2:
            base = (other, own)[turn]
            for i in range(2):
                remote(
                    acc.at[4 * (1 - core) + base + i], half.at[base + i],
                    core_send.at[2 * turn + i], core_recv.at[2 * turn + i], buddy,
                ).start()
                left_with(half.at[0], core_send.at[2 * turn + i])

    from_z(0)
    from_z(1)
    from_z(2)
    from_z(3)
    arrived(got_h.at[pl.ds(1, NZ - 1)], zh_recv)
    for step in range(1, NY):
        remote(
            got_h, got_yh.at[NY - step - 1], yh_send.at[step], yh_recv.at[NY - step - 1],
            at((y + step) % NY, z, core),
        ).start()
        left_with(got_h, yh_send.at[step])
    for y_from in range(NY):
        arrived(part_y.at[y_from], py_recv.at[y_from])
    mine_z[...] = (part_y[0] + part_y[1]) + (part_y[2] + part_y[3])
    for step in range(1, NZ):
        remote(
            mine_z, part_z.at[z], pz_send.at[step], pz_recv.at[z], at(y, (z + step) % NZ, core)
        ).start()
        left_with(mine_z, pz_send.at[step])
    pltpu.make_async_copy(mine_z, part_z.at[z], pz_recv.at[z]).start()
    from_y(1, 0)
    from_y(1, 1)
    add_rows(0, first=True, places=range(NZ // 2))
    add_rows(1, places=range(NZ // 2))
    from_y(3, 0)
    from_y(3, 1)
    add_rows(3, places=range(NZ // 2))
    from_y(2, 0)
    from_y(2, 1)
    add_rows(2, places=range(NZ // 2))
    add_rows(0, places=range(NZ // 2, NZ))
    from_y(1, 2)
    from_y(1, 3)
    add_rows(1, places=range(NZ // 2, NZ))
    from_y(3, 2)
    from_y(3, 3)
    add_rows(3, places=range(NZ // 2, NZ))
    from_y(2, 2)
    from_y(2, 3)
    add_rows(2, places=range(NZ // 2, NZ), after=to_buddy)
    for step in range(1, NY):
        left_with(got_y.at[0], y_send.at[step])
    for side in range(2):
        left_with(got_x.at[pl.ds(0, 2)], x_send.at[side])

    sibling = at(y, z + 1 - 2 * (z % 2), core)
    for i in range(2):
        arrived(half.at[other + i], core_recv.at[i])
        deep[other + i] = acc[4 * core + other + i] + half[other + i]
        remote(deep.at[other + i], sib.at[i], sib_send.at[i], sib_recv.at[i], sibling).start()
        left_with(sib.at[i], sib_send.at[i])
    for i in range(2):
        arrived(half.at[own + i], core_recv.at[2 + i])
        deep[own + i] = acc[4 * core + own + i] + half[own + i]

    def hand_over(src, dst, send, recv, row_to):
        @pl.when(row_to != row)
        def _():
            remote(src, dst, send, recv, row_to).start()

        @pl.when(row_to == row)
        def _():
            pltpu.make_async_copy(src, dst, recv).start()

        def leave():
            @pl.when(row_to != row)
            def _():
                arrived(src, send)

        leaving.append(leave)

    spot3 = 2 * core + block % 2
    for i in range(4):
        gain3[i] = gains_of(deep[i])
    for i in range(4):
        row_to = 8 * z + 4 * (block // 2) + (i + 2 * core) % 4
        hand_over(gain3.at[i], home3.at[spot3], g3_send.at[i], g3_recv.at[spot3], row_to)

    for z_from in range(NZ):
        arrived(part_z.at[z_from], pz_recv.at[z_from])
    total_z = part_z[0]
    for z_from in range(1, NZ):
        total_z = total_z + part_z[z_from]
    mine_x[...] = total_z
    here = 2 * x + core
    for step in range(1, 2 * NX):
        remote(
            mine_x, part_x.at[here], px_send.at[step], px_recv.at[here],
            at(y, z, (core + step) % 2), (x + step // 2) % NX,
        ).start()
        left_with(mine_x, px_send.at[step])
    pltpu.make_async_copy(mine_x, part_x.at[here], px_recv.at[here]).start()

    high_bits = [(2 * (own + i) + 5 * core) % 8 for i in range(2)]
    which1 = (z // 2) % 2
    for i in range(2):
        arrived(sib.at[i], sib_recv.at[i])
        mid[i] = deep[own + i] + sib[i]
        hand_over(
            mid.at[i], low.at[which1], low_send.at[i], low_recv.at[which1],
            at(2 * upper + block // 2, high_bits[i], block % 2),
        )
    spot2 = block % 2
    for i in range(2):
        gain2[i] = gains_of(mid[i])
        hand_over(
            gain2.at[i], home2.at[spot2], g2_send.at[i], g2_recv.at[spot2],
            16 * (z // 2) + 8 * (block // 2) + high_bits[i],
        )

    for i in range(4):
        arrived(home3.at[i], g3_recv.at[i])
        out_ref[i:i + 1, :] = home3[i]

    for i in range(2 * NX):
        arrived(part_x.at[i], px_recv.at[i])
    total_x = part_x[0]
    for i in range(1, 2 * NX):
        total_x = total_x + part_x[i]
    scores = -total_x[0:8] / jnp.sqrt(total_x[8:16] + penalty)
    out_ref[8:12, :] = scores[0:4]
    out_ref[12:14, :] = jnp.where(z < NZ // 2, scores[4:6], scores[6:8])

    for i in range(2):
        arrived(low.at[i], low_recv.at[i])
    last = gains_of(low[0] + low[1])
    out_ref[6:7, :] = last
    for i in range(2):
        arrived(home2.at[i], g2_recv.at[i])
        out_ref[4 + i:5 + i, :] = home2[i]

    for leave in leaving:
        leave()


def spread(all_ref, one_ref, two_ref, three_ref, child_out):
    for first, ref in ((0, three_ref), (4, two_ref), (6, one_ref)):
        for i in range(ref.shape[0] // 2):
            ref[2 * i:2 * i + 1, :] = all_ref[first + i:first + i + 1, 0:BINS]
            ref[2 * i + 1:2 * i + 2, :] = all_ref[first + i:first + i + 1, BINS:2 * BINS]
    for level in range(LEVELS):
        child_out[level, 0] = all_ref[8 + 2 * level:10 + 2 * level, :]


def on_device(gradients, hessians, bin_words, children, split_feature, split_bin):
    dma = pltpu.SemaphoreType.DMA
    vmem = pl.BlockSpec(memory_space=pltpu.VMEM)
    together = pl.pallas_call(
        kernel,
        out_shape=jax.ShapeDtypeStruct((16, 128), F32),
        in_specs=[pl.BlockSpec(memory_space=pl.ANY)] * 6,
        out_specs=vmem,
        scratch_shapes=[
            pltpu.SMEM((SPLITS,), jnp.int32),
            pltpu.SMEM((SPLITS,), jnp.int32),
            pltpu.VMEM((ROW_DEV, OUT), BF16),
            pltpu.VMEM((ROW_DEV,), BF16),
            pltpu.VMEM((32, ROW_DEV), jnp.int32),
            pltpu.VMEM((LEVELS, ROW_DEV), jnp.int32),
            pltpu.VMEM((NZ, PIECE, SLOTS), BF16),
            pltpu.VMEM((NZ, 1, SLOTS), F32),
            pltpu.VMEM((NZ - 1, PIECE, SLOTS), BF16),
            pltpu.VMEM((NZ, 1, SLOTS), F32),
            pltpu.VMEM((NY - 1, NZ, GOES_Y, SLOTS), BF16),
            pltpu.VMEM((NY - 1, NZ, 1, SLOTS), F32),
            pltpu.VMEM((NY, NZ, HALF, SLOTS), BF16),
            pltpu.VMEM((16, NZ * SLOTS), F32),
            pltpu.VMEM((8, KEEP, 128), F32),
            pltpu.VMEM((4, KEEP, 128), F32),
            pltpu.VMEM((4, KEEP, 128), F32),
            pltpu.VMEM((2, KEEP, 128), F32),
            pltpu.VMEM((2, KEEP, 128), F32),
            pltpu.VMEM((2, KEEP, 128), F32),
            pltpu.VMEM((4, 1, 128), F32),
            pltpu.VMEM((4, 1, 128), F32),
            pltpu.VMEM((2, 1, 128), F32),
            pltpu.VMEM((2, 1, 128), F32),
            pltpu.VMEM((NY, 16, 128), F32),
            pltpu.VMEM((NY, 16, 128), F32),
            pltpu.VMEM((16, 128), F32),
            pltpu.VMEM((NZ, 16, 128), F32),
            pltpu.VMEM((16, 128), F32),
            pltpu.VMEM((2 * NX, 16, 128), F32),
            dma((6,)), dma((NZ,)), dma((NZ,)), dma, dma, dma((NY,)), dma((NY - 1, 4)),
            dma((NY,)), dma((NY - 1,)), dma((2,)), dma((NY, 2)),
            dma((4,)), dma((4,)), dma((2,)), dma((2,)),
            dma((2,)), dma((2,)), dma((4,)), dma((4,)), dma((2,)), dma((2,)),
            dma((NY,)), dma((NY,)), dma((NZ,)), dma((NZ,)), dma((2 * NX,)), dma((2 * NX,)),
        ],
        compiler_params=pltpu.CompilerParams(collective_id=0, has_side_effects=True),
    )(split_feature, split_bin, gradients, hessians, bin_words, children)
    return pl.pallas_call(
        spread,
        out_shape=(
            jax.ShapeDtypeStruct((2, BINS), F32),
            jax.ShapeDtypeStruct((4, BINS), F32),
            jax.ShapeDtypeStruct((8, BINS), F32),
            jax.ShapeDtypeStruct((LEVELS, 1, 2, OUT), F32),
        ),
        in_specs=[vmem],
        out_specs=(vmem,) * 4,
    )(together)


def solution(mesh):
    placed = (P("rows", None), P("rows"), P("feat", "rows"), P(None, "rows"), P(), P())
    return jax.shard_map(
        on_device,
        mesh=mesh,
        in_specs=placed,
        out_specs=(
            P("rows", "feat"),
            P("rows", "feat"),
            P("rows", "feat"),
            P(None, "rows", None, None),
        ),
        check_vma=False,
    )
```

```python
import jax
import jax.numpy as jnp
from jax import lax
from jax.experimental import pallas as pl
from jax.experimental.pallas import tpu as pltpu
from jax.sharding import PartitionSpec as P

BINS = 64
OUT = 128
LEVELS = 3
SPLITS = 14
ROW_DEV = 512
SLOTS = 128
NY, NZ, NX = 4, 8, 4
HALF = OUT // 2
PIECE = HALF + 64
GOES_Y = HALF + 16
KEEP = OUT + 8
MESH = pl.DeviceIdType.MESH
F32 = jnp.float32
BF16 = jnp.bfloat16

penalty = 1.0
DIRECT = (0, 1, 2, 3)
NEAR = (0, 1, 7, 2, 6, 4, 3, 5)


def block_of(y, upper):
    block = 2 * (((y + 1) // 2) % 2) + y // 2
    return block + upper * (3 - 2 * block)


def nt_dot(left, right):
    return lax.dot_general(left, right, (((1,), (1,)), ((), ())), preferred_element_type=F32)


def ones_where(condition):
    return condition.astype(F32).astype(BF16)


def gains_of(left):
    total = jnp.broadcast_to(left[:, 127:128], left.shape)
    right = total - left

    def term(part):
        square = part[:OUT] * part[:OUT]
        return jnp.sum(square, axis=0, keepdims=True) / (part[OUT:OUT + 1] + penalty)

    return (term(left) + term(right) - term(total)) / OUT


def kernel(
    split_feature_any, split_bin_any, grad_any, hess_any, word_any, child_any,
    out_ref,
    split_feature, split_bin, grad_ref, hess_ref, word_ref, child_ref,
    sent, sent_h, got_z, got_h, got_y, got_yh, got_x, codes_here,
    acc, half, deep, sib, mid, low,
    gain3, home3, gain2, home2, part, part_y, mine_z, part_z, mine_x, part_x,
    in_sem, z_send, z_recv, zh_send, zh_recv, y_send, y_recv, yh_send, yh_recv,
    x_send, x_recv, core_send, core_recv, sib_send, sib_recv,
    low_send, low_recv, g3_send, g3_recv, g2_send, g2_recv,
    py_send, py_recv, pz_send, pz_recv, px_send, px_recv,
):
    row = lax.axis_index("rows")
    x = lax.axis_index("feat")
    core = row % 2
    z = (row // 2) % NZ
    y = row // 16
    upper = z // 4
    block = block_of(y, upper)
    kind = (z + upper) % 2
    own = 2 * kind
    other = 2 - own
    leaving = []

    def at(y_to, z_to, core_to):
        return y_to * 16 + z_to * 2 + core_to

    def remote(src, dst, send, recv, row_to, x_to=None):
        return pltpu.make_async_remote_copy(
            src_ref=src, dst_ref=dst, send_sem=send, recv_sem=recv,
            device_id=(row_to, x if x_to is None else x_to), device_id_type=MESH,
        )

    def arrived(ref, sem):
        pltpu.make_async_copy(ref, ref, sem).wait()

    def left_with(ref, sem):
        leaving.append(lambda: arrived(ref, sem))

    inputs = [
        pltpu.make_async_copy(src, dst, in_sem.at[i])
        for i, (src, dst) in enumerate((
            (child_any, child_ref), (hess_any, hess_ref), (word_any, word_ref),
            (grad_any, grad_ref), (split_feature_any, split_feature), (split_bin_any, split_bin),
        ))
    ]
    for copy in inputs:
        copy.start()

    barrier = pltpu.get_barrier_semaphore()

    def greet(row_to, x_to):
        pl.semaphore_signal(barrier, inc=1, device_id=(row_to, x_to), device_id_type=MESH)

    for step in (4, 3, 5, 2, 6, 1, 7):
        greet(at(y, (z + step) % NZ, core), x)
    for step in (2, 1, 3):
        greet(at((y + step) % NY, z, core), x)
    for step in (2, 1, 3):
        for side in (1, NX - 1):
            greet(at((y + step) % NY, z, core), (x + side) % NX)
    for step in range(1, 2 * NX):
        greet(at(y, z, (core + step) % 2), (x + step // 2) % NX)
    for copy in inputs:
        copy.wait()

    child = child_ref[...]
    node1 = child[0:1]
    node2 = node1 * 2 + child[1:2]
    node3 = node2 * 2 + child[2:3]
    at_node = (lax.broadcasted_iota(jnp.int32, (8, ROW_DEV), 0) == node3).astype(F32)
    upto = ones_where(
        lax.broadcasted_iota(jnp.int32, (ROW_DEV, ROW_DEV), 0)
        <= lax.broadcasted_iota(jnp.int32, (ROW_DEV, ROW_DEV), 1)
    )
    running = jnp.dot(at_node.astype(BF16), upto, preferred_element_type=F32)
    rank = jnp.sum(at_node * running, axis=0, keepdims=True).astype(jnp.int32) - 1
    slot = node3 * SLOTS + rank

    hess = hess_ref[...].reshape(1, ROW_DEV).astype(F32)
    outputs_all = grad_ref[...].astype(F32).T
    outputs_half = jnp.where(x % 2 == 0, outputs_all[:HALF], outputs_all[HALF:]).astype(BF16)
    words = word_ref[...]
    natural = jnp.concatenate(
        [jnp.bitwise_and(words, 63), jnp.bitwise_and(jnp.right_shift(words, 6), 63)], 0
    ).astype(F32).astype(BF16)
    spot64 = lax.broadcasted_iota(jnp.int32, (64, 1), 0)
    source64 = (
        32 * jnp.bitwise_and(jnp.right_shift(spot64, 3), 1)
        + 16 * jnp.right_shift(spot64, 5)
        + 2 * jnp.bitwise_and(spot64, 7)
        + jnp.bitwise_and(jnp.right_shift(spot64, 4), 1)
    )
    moved = ones_where(lax.broadcasted_iota(jnp.int32, (64, 64), 1) == source64)
    code_rows = jnp.dot(moved, natural, preferred_element_type=F32).astype(BF16)
    hess_tile = jnp.concatenate([hess, jnp.zeros((15, ROW_DEV), F32)], 0).astype(BF16)
    packed = jnp.concatenate([outputs_half, code_rows, hess_tile], 0)
    for pair in range(NZ // 2):
        wanted = lax.broadcasted_iota(jnp.int32, (2 * SLOTS, ROW_DEV), 0) + pair * 2 * SLOTS
        chosen = nt_dot(packed, ones_where(wanted == slot))
        for side in range(2):
            lanes = slice(side * SLOTS, (side + 1) * SLOTS)
            sent[2 * pair + side] = chosen[:PIECE, lanes].astype(BF16)
            sent_h[2 * pair + side] = chosen[PIECE:PIECE + 1, lanes]
    got_h[0] = sent_h[z]

    pl.semaphore_wait(barrier, (NZ - 1) + 3 * (NY - 1) + (2 * NX - 1))
    for step in (1, 7, 4, 2, 6, 3, 5):
        z_to = (z + step) % NZ
        place = NEAR.index((NZ - step) % NZ)
        remote(
            sent.at[z_to], got_z.at[place - 1], z_send.at[step], z_recv.at[place], at(y, z_to, core)
        ).start()
        left_with(sent.at[step], z_send.at[step])
    for step in (1, 7, 4, 2, 6, 3, 5):
        z_to = (z + step) % NZ
        place = NEAR.index((NZ - step) % NZ)
        remote(
            sent_h.at[z_to], got_h.at[place], zh_send, zh_recv, at(y, z_to, core)
        ).start()
    left_with(got_h.at[pl.ds(1, NZ - 1)], zh_send)

    rows32 = lax.broadcasted_iota(jnp.int32, (32, 1), 0)
    yy = jnp.right_shift(rows32, 3)
    which = jnp.bitwise_and(jnp.right_shift(rows32, 1), 3)
    right_side = jnp.bitwise_and(rows32, 1)
    is_one, is_two = which == 0, which == 1
    node_row = jnp.where(
        is_one, jnp.right_shift(yy, 1), jnp.where(is_two, yy, 2 * yy + which - 2)
    )
    split_row = node_row + jnp.where(is_one, 0, jnp.where(is_two, 2, 6))
    feature_row = jnp.zeros((32, 1), jnp.int32)
    bin_row = jnp.zeros((32, 1), jnp.int32)
    for s in range(SPLITS):
        feature_row = jnp.where(split_row == s, split_feature[s], feature_row)
        bin_row = jnp.where(split_row == s, split_bin[s], bin_row)
    inner = jnp.bitwise_and(feature_row, 63)
    place = (
        32 * jnp.right_shift(inner, 5)
        + 16 * jnp.bitwise_and(jnp.right_shift(inner, 1), 1)
        + 8 * jnp.bitwise_and(inner, 1)
        + jnp.bitwise_and(jnp.right_shift(inner, 2), 7)
    )
    panel_row = jnp.right_shift(feature_row, 6)
    spot = ones_where(lax.broadcasted_iota(jnp.int32, (32, 64), 1) == place)
    code_row = jnp.dot(spot, code_rows, preferred_element_type=F32).astype(jnp.int32)
    node_here = jnp.where(is_one, node1, jnp.where(is_two, node2, node3))
    goes_right = (code_row > bin_row).astype(jnp.int32)
    wanted_row = (node_here == node_row) & (panel_row == x) & (goes_right == right_side)
    wanted_row = wanted_row.astype(F32)
    sums = jnp.dot(wanted_row.astype(BF16), grad_ref[...], preferred_element_type=F32)
    sums_h = jnp.sum(wanted_row * hess, axis=1, keepdims=True)
    for y_to in range(NY):
        part[y_to, 0:8] = sums[8 * y_to:8 * y_to + 8]
        part[y_to, 8:16] = jnp.broadcast_to(sums_h[8 * y_to:8 * y_to + 8], (8, OUT))
    for step in range(1, NY):
        y_to = (y + step) % NY
        remote(
            part.at[y_to], part_y.at[y], py_send.at[step], py_recv.at[y], at(y_to, z, core)
        ).start()
        left_with(part.at[step], py_send.at[step])
    pltpu.make_async_copy(part.at[y], part_y.at[y], py_recv.at[y]).start()

    def piece(place):
        return sent.at[z] if place == 0 else got_z.at[place - 1]

    def to_x(src, offset, place, y_step=0):
        step = 1 - 2 * (place % 2)
        late = int(place >= NZ // 2)
        remote(
            src, got_x.at[offset, place], x_send.at[place % 2], x_recv.at[offset, late],
            at((y + y_step) % NY, z, core), (x + step) % NX,
        ).start()

    def from_z(group):
        for place in (2 * group, 2 * group + 1):
            if place:
                arrived(got_z.at[place - 1], z_recv.at[place])
            here = piece(place)
            for step in (1, 3, 2):
                remote(
                    here.at[pl.ds(0, HALF)], got_y.at[NY - step - 1, place, pl.ds(0, HALF)],
                    y_send.at[step], y_recv.at[NY - step - 1, group],
                    at((y + step) % NY, z, core),
                ).start()
            for step in (1, 3, 2):
                y_to = (y + step) % NY
                start = pl.multiple_of(HALF + 16 * block_of(y_to, upper), 16)
                remote(
                    here.at[pl.ds(start, 16)], got_y.at[NY - step - 1, place, pl.ds(HALF, 16)],
                    y_send.at[step], y_recv.at[NY - step - 1, group], at(y_to, z, core),
                ).start()
            for step in (0, 1, 3, 2) if group in DIRECT else (0,):
                to_x(here.at[pl.ds(0, HALF)], (NY - step) % NY, place, step)

    def from_y(offset, group):
        arrived(got_y.at[offset - 1, pl.ds(2 * group, 2)], y_recv.at[offset - 1, group])
        for place in (2 * group, 2 * group + 1) if group not in DIRECT else ():
            to_x(got_y.at[offset - 1, place, pl.ds(0, HALF)], offset, place)

    bins = lax.broadcasted_iota(jnp.int32, (BINS, 1), 0).astype(F32)

    def add_rows(offset, first=False, after=None, places=range(NZ)):
        here_x = pl.ds(places[0], len(places))
        late = int(places[0] > 0)
        arrived(got_x.at[offset, here_x], x_recv.at[offset, late])
        if offset == 0:
            pieces = [piece(i) for i in places]
            start = pl.multiple_of(HALF + 16 * block, 16)
            kept = [ref[0:HALF, :] for ref in pieces]
            codes = [ref[pl.ds(start, 16), :] for ref in pieces]
            weights = [got_h[i] for i in places]
        else:
            if not late:
                arrived(got_yh.at[offset - 1], yh_recv.at[offset - 1])
            kept = [got_y[offset - 1, i, 0:HALF, :] for i in places]
            codes = [got_y[offset - 1, i, HALF:GOES_Y, :] for i in places]
            weights = [got_yh[offset - 1, i] for i in places]
        tile = jnp.concatenate(
            [jnp.concatenate(weights, 1), jnp.zeros((15, len(places) * SLOTS), F32)], 0
        ).astype(BF16)
        values = jnp.concatenate([
            jnp.concatenate(kept, 1),
            jnp.concatenate([got_x[offset, i] for i in places], 1),
            tile,
        ], 0)
        codes_here[:, 0:len(places) * SLOTS] = jnp.concatenate(codes, 1).astype(F32)
        for turn, (core_to, base) in enumerate(
            ((1 - core, other), (1 - core, own), (core, other), (core, own))
        ):
            masks = []
            for i in range(2):
                high = (2 * (base + i) + 5 * core_to) % 8
                for line in (high, 8 + high):
                    masks.append(ones_where(codes_here[pl.ds(line, 1), 0:len(places) * SLOTS] <= bins))
            found = nt_dot(values, jnp.concatenate(masks, 0))
            for i in range(2):
                new = found[:KEEP, 128 * i:128 * i + 128]
                if first:
                    acc[4 * core_to + base + i] = new
                else:
                    acc[4 * core_to + base + i] += new
            if after is not None:
                after(turn)

    buddy = at(y, z, 1 - core)

    def to_buddy(turn):
        if turn < 2:
            base = (other, own)[turn]
            for i in range(2):
                remote(
                    acc.at[4 * (1 - core) + base + i], half.at[base + i],
                    core_send.at[2 * turn + i], core_recv.at[2 * turn + i], buddy,
                ).start()
                left_with(half.at[0], core_send.at[2 * turn + i])

    from_z(0)
    from_z(1)
    from_z(2)
    from_z(3)
    arrived(got_h.at[pl.ds(1, NZ - 1)], zh_recv)
    for step in range(1, NY):
        remote(
            got_h, got_yh.at[NY - step - 1], yh_send.at[step], yh_recv.at[NY - step - 1],
            at((y + step) % NY, z, core),
        ).start()
        left_with(got_h, yh_send.at[step])
    for y_from in range(NY):
        arrived(part_y.at[y_from], py_recv.at[y_from])
    mine_z[...] = (part_y[0] + part_y[1]) + (part_y[2] + part_y[3])
    for step in range(1, NZ):
        remote(
            mine_z, part_z.at[z], pz_send.at[step], pz_recv.at[z], at(y, (z + step) % NZ, core)
        ).start()
        left_with(mine_z, pz_send.at[step])
    pltpu.make_async_copy(mine_z, part_z.at[z], pz_recv.at[z]).start()
    from_y(1, 0)
    from_y(1, 1)
    add_rows(0, first=True, places=range(NZ // 2))
    add_rows(1, places=range(NZ // 2))
    from_y(3, 0)
    from_y(3, 1)
    add_rows(3, places=range(NZ // 2))
    from_y(2, 0)
    from_y(2, 1)
    add_rows(2, places=range(NZ // 2))
    add_rows(0, places=range(NZ // 2, NZ))
    from_y(1, 2)
    from_y(1, 3)
    add_rows(1, places=range(NZ // 2, NZ))
    from_y(3, 2)
    from_y(3, 3)
    add_rows(3, places=range(NZ // 2, NZ))
    from_y(2, 2)
    from_y(2, 3)
    add_rows(2, places=range(NZ // 2, NZ), after=to_buddy)
    for step in range(1, NY):
        left_with(got_y.at[0], y_send.at[step])
    for side in range(2):
        left_with(got_x.at[pl.ds(0, 2)], x_send.at[side])

    sibling = at(y, z + 1 - 2 * (z % 2), core)
    for i in range(2):
        arrived(half.at[other + i], core_recv.at[i])
        deep[other + i] = acc[4 * core + other + i] + half[other + i]
        remote(deep.at[other + i], sib.at[i], sib_send.at[i], sib_recv.at[i], sibling).start()
        left_with(sib.at[i], sib_send.at[i])
    for i in range(2):
        arrived(half.at[own + i], core_recv.at[2 + i])
        deep[own + i] = acc[4 * core + own + i] + half[own + i]

    def hand_over(src, dst, send, recv, row_to):
        @pl.when(row_to != row)
        def _():
            remote(src, dst, send, recv, row_to).start()

        @pl.when(row_to == row)
        def _():
            pltpu.make_async_copy(src, dst, recv).start()

        def leave():
            @pl.when(row_to != row)
            def _():
                arrived(src, send)

        leaving.append(leave)

    spot3 = 2 * core + block % 2
    for i in range(4):
        gain3[i] = gains_of(deep[i])
    for i in range(4):
        row_to = 8 * z + 4 * (block // 2) + (i + 2 * core) % 4
        hand_over(gain3.at[i], home3.at[spot3], g3_send.at[i], g3_recv.at[spot3], row_to)

    for z_from in range(NZ):
        arrived(part_z.at[z_from], pz_recv.at[z_from])
    total_z = part_z[0]
    for z_from in range(1, NZ):
        total_z = total_z + part_z[z_from]
    mine_x[...] = total_z
    here = 2 * x + core
    for step in range(1, 2 * NX):
        remote(
            mine_x, part_x.at[here], px_send.at[step], px_recv.at[here],
            at(y, z, (core + step) % 2), (x + step // 2) % NX,
        ).start()
        left_with(mine_x, px_send.at[step])
    pltpu.make_async_copy(mine_x, part_x.at[here], px_recv.at[here]).start()

    high_bits = [(2 * (own + i) + 5 * core) % 8 for i in range(2)]
    which1 = (z // 2) % 2
    for i in range(2):
        arrived(sib.at[i], sib_recv.at[i])
        mid[i] = deep[own + i] + sib[i]
        hand_over(
            mid.at[i], low.at[which1], low_send.at[i], low_recv.at[which1],
            at(2 * upper + block // 2, high_bits[i], block % 2),
        )
    spot2 = block % 2
    for i in range(2):
        gain2[i] = gains_of(mid[i])
        hand_over(
            gain2.at[i], home2.at[spot2], g2_send.at[i], g2_recv.at[spot2],
            16 * (z // 2) + 8 * (block // 2) + high_bits[i],
        )

    for i in range(4):
        arrived(home3.at[i], g3_recv.at[i])
        out_ref[i:i + 1, :] = home3[i]

    for i in range(2 * NX):
        arrived(part_x.at[i], px_recv.at[i])
    total_x = part_x[0]
    for i in range(1, 2 * NX):
        total_x = total_x + part_x[i]
    scores = -total_x[0:8] / jnp.sqrt(total_x[8:16] + penalty)
    out_ref[8:12, :] = scores[0:4]
    out_ref[12:14, :] = jnp.where(z < NZ // 2, scores[4:6], scores[6:8])

    for i in range(2):
        arrived(low.at[i], low_recv.at[i])
    last = gains_of(low[0] + low[1])
    out_ref[6:7, :] = last
    for i in range(2):
        arrived(home2.at[i], g2_recv.at[i])
        out_ref[4 + i:5 + i, :] = home2[i]

    for leave in leaving:
        leave()


def spread(all_ref, one_ref, two_ref, three_ref, child_out):
    for first, ref in ((0, three_ref), (4, two_ref), (6, one_ref)):
        for i in range(ref.shape[0] // 2):
            ref[2 * i:2 * i + 1, :] = all_ref[first + i:first + i + 1, 0:BINS]
            ref[2 * i + 1:2 * i + 2, :] = all_ref[first + i:first + i + 1, BINS:2 * BINS]
    for level in range(LEVELS):
        child_out[level, 0] = all_ref[8 + 2 * level:10 + 2 * level, :]


def on_device(gradients, hessians, bin_words, children, split_feature, split_bin):
    dma = pltpu.SemaphoreType.DMA
    vmem = pl.BlockSpec(memory_space=pltpu.VMEM)
    together = pl.pallas_call(
        kernel,
        out_shape=pltpu.VMEM((16, 128), F32),
        in_specs=[pl.BlockSpec(memory_space=pl.ANY)] * 6,
        out_specs=vmem,
        scratch_shapes=[
            pltpu.SMEM((SPLITS,), jnp.int32),
            pltpu.SMEM((SPLITS,), jnp.int32),
            pltpu.VMEM((ROW_DEV, OUT), BF16),
            pltpu.VMEM((ROW_DEV,), BF16),
            pltpu.VMEM((32, ROW_DEV), jnp.int32),
            pltpu.VMEM((LEVELS, ROW_DEV), jnp.int32),
            pltpu.VMEM((NZ, PIECE, SLOTS), BF16),
            pltpu.VMEM((NZ, 1, SLOTS), F32),
            pltpu.VMEM((NZ - 1, PIECE, SLOTS), BF16),
            pltpu.VMEM((NZ, 1, SLOTS), F32),
            pltpu.VMEM((NY - 1, NZ, GOES_Y, SLOTS), BF16),
            pltpu.VMEM((NY - 1, NZ, 1, SLOTS), F32),
            pltpu.VMEM((NY, NZ, HALF, SLOTS), BF16),
            pltpu.VMEM((16, NZ * SLOTS), F32),
            pltpu.VMEM((8, KEEP, 128), F32),
            pltpu.VMEM((4, KEEP, 128), F32),
            pltpu.VMEM((4, KEEP, 128), F32),
            pltpu.VMEM((2, KEEP, 128), F32),
            pltpu.VMEM((2, KEEP, 128), F32),
            pltpu.VMEM((2, KEEP, 128), F32),
            pltpu.VMEM((4, 1, 128), F32),
            pltpu.VMEM((4, 1, 128), F32),
            pltpu.VMEM((2, 1, 128), F32),
            pltpu.VMEM((2, 1, 128), F32),
            pltpu.VMEM((NY, 16, 128), F32),
            pltpu.VMEM((NY, 16, 128), F32),
            pltpu.VMEM((16, 128), F32),
            pltpu.VMEM((NZ, 16, 128), F32),
            pltpu.VMEM((16, 128), F32),
            pltpu.VMEM((2 * NX, 16, 128), F32),
            dma((6,)), dma((NZ,)), dma((NZ,)), dma, dma, dma((NY,)), dma((NY - 1, 4)),
            dma((NY,)), dma((NY - 1,)), dma((2,)), dma((NY, 2)),
            dma((4,)), dma((4,)), dma((2,)), dma((2,)),
            dma((2,)), dma((2,)), dma((4,)), dma((4,)), dma((2,)), dma((2,)),
            dma((NY,)), dma((NY,)), dma((NZ,)), dma((NZ,)), dma((2 * NX,)), dma((2 * NX,)),
        ],
        compiler_params=pltpu.CompilerParams(collective_id=0, has_side_effects=True),
    )(split_feature, split_bin, gradients, hessians, bin_words, children)
    together = pltpu.with_memory_space_constraint(together, pltpu.VMEM)
    return pl.pallas_call(
        spread,
        out_shape=(
            jax.ShapeDtypeStruct((2, BINS), F32),
            jax.ShapeDtypeStruct((4, BINS), F32),
            jax.ShapeDtypeStruct((8, BINS), F32),
            jax.ShapeDtypeStruct((LEVELS, 1, 2, OUT), F32),
        ),
        in_specs=[vmem],
        out_specs=(vmem,) * 4,
    )(together)


def solution(mesh):
    placed = (P("rows", None), P("rows"), P("feat", "rows"), P(None, "rows"), P(), P())
    return jax.shard_map(
        on_device,
        mesh=mesh,
        in_specs=placed,
        out_specs=(
            P("rows", "feat"),
            P("rows", "feat"),
            P("rows", "feat"),
            P(None, "rows", None, None),
        ),
        check_vma=False,
    )
```

```python
import jax
import jax.numpy as jnp
from jax import lax
from jax.experimental import pallas as pl
from jax.experimental.pallas import tpu as pltpu
from jax.sharding import PartitionSpec as P

BINS = 64
OUT = 128
LEVELS = 3
SPLITS = 14
ROW_DEV = 512
SLOTS = 128
NY, NZ, NX = 4, 8, 4
HALF = OUT // 2
PIECE = HALF + 64
GOES_Y = HALF + 16
KEEP = OUT + 8
MESH = pl.DeviceIdType.MESH
F32 = jnp.float32
BF16 = jnp.bfloat16

penalty = 1.0
DIRECT = (0, 1, 2, 3)
NEAR = (0, 1, 7, 2, 6, 4, 3, 5)


def block_of(y, upper):
    block = 2 * (((y + 1) // 2) % 2) + y // 2
    return block + upper * (3 - 2 * block)


def nt_dot(left, right):
    return lax.dot_general(left, right, (((1,), (1,)), ((), ())), preferred_element_type=F32)


def ones_where(condition):
    return condition.astype(F32).astype(BF16)


def gains_of(left):
    total = jnp.broadcast_to(left[:, 127:128], left.shape)
    right = total - left

    def term(part):
        square = part[:OUT] * part[:OUT]
        return jnp.sum(square, axis=0, keepdims=True) / (part[OUT:OUT + 1] + penalty)

    return (term(left) + term(right) - term(total)) / OUT


def kernel(
    split_feature_any, split_bin_any, grad_any, hess_any, word_any, child_any,
    out_ref,
    split_feature, split_bin, grad_ref, hess_ref, word_ref, child_ref,
    sent, sent_h, got_z, got_h, got_y, got_yh, got_x, codes_here,
    acc, half, deep, sib, mid, low,
    gain3, home3, gain2, home2, part, part_y, mine_z, part_z, mine_x, part_x,
    in_sem, z_send, z_recv, zh_send, zh_recv, y_send, y_recv, yh_send, yh_recv,
    x_send, x_recv, core_send, core_recv, sib_send, sib_recv,
    low_send, low_recv, g3_send, g3_recv, g2_send, g2_recv,
    py_send, py_recv, pz_send, pz_recv, px_send, px_recv,
):
    row = lax.axis_index("rows")
    x = lax.axis_index("feat")
    core = row % 2
    z = (row // 2) % NZ
    y = row // 16
    upper = z // 4
    block = block_of(y, upper)
    kind = (z + upper) % 2
    own = 2 * kind
    other = 2 - own
    leaving = []

    def at(y_to, z_to, core_to):
        return y_to * 16 + z_to * 2 + core_to

    def remote(src, dst, send, recv, row_to, x_to=None):
        return pltpu.make_async_remote_copy(
            src_ref=src, dst_ref=dst, send_sem=send, recv_sem=recv,
            device_id=(row_to, x if x_to is None else x_to), device_id_type=MESH,
        )

    def arrived(ref, sem):
        pltpu.make_async_copy(ref, ref, sem).wait()

    def left_with(ref, sem):
        leaving.append(lambda: arrived(ref, sem))

    inputs = [
        pltpu.make_async_copy(src, dst, in_sem.at[i])
        for i, (src, dst) in enumerate((
            (child_any, child_ref), (hess_any, hess_ref), (word_any, word_ref),
            (grad_any, grad_ref), (split_feature_any, split_feature), (split_bin_any, split_bin),
        ))
    ]
    for copy in inputs:
        copy.start()

    barrier = pltpu.get_barrier_semaphore()

    def greet(row_to, x_to):
        pl.semaphore_signal(barrier, inc=1, device_id=(row_to, x_to), device_id_type=MESH)

    for step in (4, 3, 5, 2, 6, 1, 7):
        greet(at(y, (z + step) % NZ, core), x)
    for step in (2, 1, 3):
        greet(at((y + step) % NY, z, core), x)
    for step in (2, 1, 3):
        for side in (1, NX - 1):
            greet(at((y + step) % NY, z, core), (x + side) % NX)
    for step in range(1, 2 * NX):
        greet(at(y, z, (core + step) % 2), (x + step // 2) % NX)
    for copy in inputs:
        copy.wait()

    child = child_ref[...]
    node1 = child[0:1]
    node2 = node1 * 2 + child[1:2]
    node3 = node2 * 2 + child[2:3]
    at_node = (lax.broadcasted_iota(jnp.int32, (8, ROW_DEV), 0) == node3).astype(F32)
    upto = ones_where(
        lax.broadcasted_iota(jnp.int32, (ROW_DEV, ROW_DEV), 0)
        <= lax.broadcasted_iota(jnp.int32, (ROW_DEV, ROW_DEV), 1)
    )
    running = jnp.dot(at_node.astype(BF16), upto, preferred_element_type=F32)
    rank = jnp.sum(at_node * running, axis=0, keepdims=True).astype(jnp.int32) - 1
    slot = node3 * SLOTS + rank

    hess = hess_ref[...].reshape(1, ROW_DEV).astype(F32)
    outputs_all = grad_ref[...].astype(F32).T
    outputs_half = jnp.where(x % 2 == 0, outputs_all[:HALF], outputs_all[HALF:]).astype(BF16)
    words = word_ref[...]
    natural = jnp.concatenate(
        [jnp.bitwise_and(words, 63), jnp.bitwise_and(jnp.right_shift(words, 6), 63)], 0
    ).astype(F32).astype(BF16)
    spot64 = lax.broadcasted_iota(jnp.int32, (64, 1), 0)
    source64 = (
        32 * jnp.bitwise_and(jnp.right_shift(spot64, 3), 1)
        + 16 * jnp.right_shift(spot64, 5)
        + 2 * jnp.bitwise_and(spot64, 7)
        + jnp.bitwise_and(jnp.right_shift(spot64, 4), 1)
    )
    moved = ones_where(lax.broadcasted_iota(jnp.int32, (64, 64), 1) == source64)
    code_rows = jnp.dot(moved, natural, preferred_element_type=F32).astype(BF16)
    hess_tile = jnp.concatenate([hess, jnp.zeros((15, ROW_DEV), F32)], 0).astype(BF16)
    packed = jnp.concatenate([outputs_half, code_rows, hess_tile], 0)
    for pair in range(NZ // 2):
        wanted = lax.broadcasted_iota(jnp.int32, (2 * SLOTS, ROW_DEV), 0) + pair * 2 * SLOTS
        chosen = nt_dot(packed, ones_where(wanted == slot))
        for side in range(2):
            lanes = slice(side * SLOTS, (side + 1) * SLOTS)
            sent[2 * pair + side] = chosen[:PIECE, lanes].astype(BF16)
            sent_h[2 * pair + side] = chosen[PIECE:PIECE + 1, lanes]
    got_h[0] = sent_h[z]

    pl.semaphore_wait(barrier, (NZ - 1) + 3 * (NY - 1) + (2 * NX - 1))
    for step in (1, 7, 4, 2, 6, 3, 5):
        z_to = (z + step) % NZ
        place = NEAR.index((NZ - step) % NZ)
        remote(
            sent.at[z_to], got_z.at[place - 1], z_send.at[step], z_recv.at[place], at(y, z_to, core)
        ).start()
        left_with(sent.at[step], z_send.at[step])
    for step in (1, 7, 4, 2, 6, 3, 5):
        z_to = (z + step) % NZ
        place = NEAR.index((NZ - step) % NZ)
        remote(
            sent_h.at[z_to], got_h.at[place], zh_send, zh_recv, at(y, z_to, core)
        ).start()
    left_with(got_h.at[pl.ds(1, NZ - 1)], zh_send)

    rows32 = lax.broadcasted_iota(jnp.int32, (32, 1), 0)
    yy = jnp.right_shift(rows32, 3)
    which = jnp.bitwise_and(jnp.right_shift(rows32, 1), 3)
    right_side = jnp.bitwise_and(rows32, 1)
    is_one, is_two = which == 0, which == 1
    node_row = jnp.where(
        is_one, jnp.right_shift(yy, 1), jnp.where(is_two, yy, 2 * yy + which - 2)
    )
    split_row = node_row + jnp.where(is_one, 0, jnp.where(is_two, 2, 6))
    feature_row = jnp.zeros((32, 1), jnp.int32)
    bin_row = jnp.zeros((32, 1), jnp.int32)
    for s in range(SPLITS):
        feature_row = jnp.where(split_row == s, split_feature[s], feature_row)
        bin_row = jnp.where(split_row == s, split_bin[s], bin_row)
    inner = jnp.bitwise_and(feature_row, 63)
    place = (
        32 * jnp.right_shift(inner, 5)
        + 16 * jnp.bitwise_and(jnp.right_shift(inner, 1), 1)
        + 8 * jnp.bitwise_and(inner, 1)
        + jnp.bitwise_and(jnp.right_shift(inner, 2), 7)
    )
    panel_row = jnp.right_shift(feature_row, 6)
    spot = ones_where(lax.broadcasted_iota(jnp.int32, (32, 64), 1) == place)
    code_row = jnp.dot(spot, code_rows, preferred_element_type=F32).astype(jnp.int32)
    node_here = jnp.where(is_one, node1, jnp.where(is_two, node2, node3))
    goes_right = (code_row > bin_row).astype(jnp.int32)
    wanted_row = (node_here == node_row) & (panel_row == x) & (goes_right == right_side)
    wanted_row = wanted_row.astype(F32)
    sums = jnp.dot(wanted_row.astype(BF16), grad_ref[...], preferred_element_type=F32)
    sums_h = jnp.sum(wanted_row * hess, axis=1, keepdims=True)
    for y_to in range(NY):
        part[y_to, 0:8] = sums[8 * y_to:8 * y_to + 8]
        part[y_to, 8:16] = jnp.broadcast_to(sums_h[8 * y_to:8 * y_to + 8], (8, OUT))
    for step in range(1, NY):
        y_to = (y + step) % NY
        remote(
            part.at[y_to], part_y.at[y], py_send.at[step], py_recv.at[y], at(y_to, z, core)
        ).start()
        left_with(part.at[step], py_send.at[step])
    pltpu.make_async_copy(part.at[y], part_y.at[y], py_recv.at[y]).start()

    def piece(place):
        return sent.at[z] if place == 0 else got_z.at[place - 1]

    def to_x(src, offset, place, y_step=0):
        step = 1 - 2 * (place % 2)
        late = int(place >= NZ // 2)
        remote(
            src, got_x.at[offset, place], x_send.at[place % 2], x_recv.at[offset, late],
            at((y + y_step) % NY, z, core), (x + step) % NX,
        ).start()

    def from_z(group):
        for place in (2 * group, 2 * group + 1):
            if place:
                arrived(got_z.at[place - 1], z_recv.at[place])
            here = piece(place)
            for step in (1, 3, 2):
                remote(
                    here.at[pl.ds(0, HALF)], got_y.at[NY - step - 1, place, pl.ds(0, HALF)],
                    y_send.at[step], y_recv.at[NY - step - 1, group],
                    at((y + step) % NY, z, core),
                ).start()
            for step in (1, 3, 2):
                y_to = (y + step) % NY
                start = pl.multiple_of(HALF + 16 * block_of(y_to, upper), 16)
                remote(
                    here.at[pl.ds(start, 16)], got_y.at[NY - step - 1, place, pl.ds(HALF, 16)],
                    y_send.at[step], y_recv.at[NY - step - 1, group], at(y_to, z, core),
                ).start()
            for step in (0, 1, 3, 2) if group in DIRECT else (0,):
                to_x(here.at[pl.ds(0, HALF)], (NY - step) % NY, place, step)

    def from_y(offset, group):
        arrived(got_y.at[offset - 1, pl.ds(2 * group, 2)], y_recv.at[offset - 1, group])
        for place in (2 * group, 2 * group + 1) if group not in DIRECT else ():
            to_x(got_y.at[offset - 1, place, pl.ds(0, HALF)], offset, place)

    bins = lax.broadcasted_iota(jnp.int32, (BINS, 1), 0).astype(F32)

    def add_rows(offset, first=False, after=None, places=range(NZ)):
        for late in range(places[0] // 4, places[-1] // 4 + 1):
            arrived(got_x.at[offset, pl.ds(4 * late, 4)], x_recv.at[offset, late])
        if offset == 0:
            pieces = [piece(i) for i in places]
            start = pl.multiple_of(HALF + 16 * block, 16)
            kept = [ref[0:HALF, :] for ref in pieces]
            codes = [ref[pl.ds(start, 16), :] for ref in pieces]
            weights = [got_h[i] for i in places]
        else:
            if places[0] == 0:
                arrived(got_yh.at[offset - 1], yh_recv.at[offset - 1])
            kept = [got_y[offset - 1, i, 0:HALF, :] for i in places]
            codes = [got_y[offset - 1, i, HALF:GOES_Y, :] for i in places]
            weights = [got_yh[offset - 1, i] for i in places]
        tile = jnp.concatenate(
            [jnp.concatenate(weights, 1), jnp.zeros((15, len(places) * SLOTS), F32)], 0
        ).astype(BF16)
        values = jnp.concatenate([
            jnp.concatenate(kept, 1),
            jnp.concatenate([got_x[offset, i] for i in places], 1),
            tile,
        ], 0)
        codes_here[:, 0:len(places) * SLOTS] = jnp.concatenate(codes, 1).astype(F32)
        for turn, (core_to, base) in enumerate(
            ((1 - core, other), (1 - core, own), (core, other), (core, own))
        ):
            masks = []
            for i in range(2):
                high = (2 * (base + i) + 5 * core_to) % 8
                for line in (high, 8 + high):
                    masks.append(ones_where(codes_here[pl.ds(line, 1), 0:len(places) * SLOTS] <= bins))
            found = nt_dot(values, jnp.concatenate(masks, 0))
            for i in range(2):
                new = found[:KEEP, 128 * i:128 * i + 128]
                if first:
                    acc[4 * core_to + base + i] = new
                else:
                    acc[4 * core_to + base + i] += new
            if after is not None:
                after(turn)

    buddy = at(y, z, 1 - core)

    def to_buddy(turn):
        if turn < 2:
            base = (other, own)[turn]
            for i in range(2):
                remote(
                    acc.at[4 * (1 - core) + base + i], half.at[base + i],
                    core_send.at[2 * turn + i], core_recv.at[2 * turn + i], buddy,
                ).start()
                left_with(half.at[0], core_send.at[2 * turn + i])

    from_z(0)
    from_z(1)
    from_z(2)
    from_z(3)
    arrived(got_h.at[pl.ds(1, NZ - 1)], zh_recv)
    for step in range(1, NY):
        remote(
            got_h, got_yh.at[NY - step - 1], yh_send.at[step], yh_recv.at[NY - step - 1],
            at((y + step) % NY, z, core),
        ).start()
        left_with(got_h, yh_send.at[step])
    for y_from in range(NY):
        arrived(part_y.at[y_from], py_recv.at[y_from])
    mine_z[...] = (part_y[0] + part_y[1]) + (part_y[2] + part_y[3])
    for step in range(1, NZ):
        remote(
            mine_z, part_z.at[z], pz_send.at[step], pz_recv.at[z], at(y, (z + step) % NZ, core)
        ).start()
        left_with(mine_z, pz_send.at[step])
    pltpu.make_async_copy(mine_z, part_z.at[z], pz_recv.at[z]).start()
    add_rows(0, first=True, places=range(0, 8))
    from_y(1, 0)
    from_y(1, 1)
    from_y(1, 2)
    from_y(1, 3)
    add_rows(1, places=range(0, 8))
    from_y(3, 0)
    from_y(3, 1)
    from_y(3, 2)
    from_y(3, 3)
    add_rows(3, places=range(0, 8))
    from_y(2, 0)
    from_y(2, 1)
    add_rows(2, places=range(0, 4))
    from_y(2, 2)
    from_y(2, 3)
    add_rows(2, places=range(4, 8), after=to_buddy)
    for step in range(1, NY):
        left_with(got_y.at[0], y_send.at[step])
    for side in range(2):
        left_with(got_x.at[pl.ds(0, 2)], x_send.at[side])

    sibling = at(y, z + 1 - 2 * (z % 2), core)
    for i in range(2):
        arrived(half.at[other + i], core_recv.at[i])
        deep[other + i] = acc[4 * core + other + i] + half[other + i]
        remote(deep.at[other + i], sib.at[i], sib_send.at[i], sib_recv.at[i], sibling).start()
        left_with(sib.at[i], sib_send.at[i])
    for i in range(2):
        arrived(half.at[own + i], core_recv.at[2 + i])
        deep[own + i] = acc[4 * core + own + i] + half[own + i]

    def hand_over(src, dst, send, recv, row_to):
        @pl.when(row_to != row)
        def _():
            remote(src, dst, send, recv, row_to).start()

        @pl.when(row_to == row)
        def _():
            pltpu.make_async_copy(src, dst, recv).start()

        def leave():
            @pl.when(row_to != row)
            def _():
                arrived(src, send)

        leaving.append(leave)

    spot3 = 2 * core + block % 2
    for i in range(4):
        gain3[i] = gains_of(deep[i])
    for i in range(4):
        row_to = 8 * z + 4 * (block // 2) + (i + 2 * core) % 4
        hand_over(gain3.at[i], home3.at[spot3], g3_send.at[i], g3_recv.at[spot3], row_to)

    for z_from in range(NZ):
        arrived(part_z.at[z_from], pz_recv.at[z_from])
    total_z = part_z[0]
    for z_from in range(1, NZ):
        total_z = total_z + part_z[z_from]
    mine_x[...] = total_z
    here = 2 * x + core
    for step in range(1, 2 * NX):
        remote(
            mine_x, part_x.at[here], px_send.at[step], px_recv.at[here],
            at(y, z, (core + step) % 2), (x + step // 2) % NX,
        ).start()
        left_with(mine_x, px_send.at[step])
    pltpu.make_async_copy(mine_x, part_x.at[here], px_recv.at[here]).start()

    high_bits = [(2 * (own + i) + 5 * core) % 8 for i in range(2)]
    which1 = (z // 2) % 2
    for i in range(2):
        arrived(sib.at[i], sib_recv.at[i])
        mid[i] = deep[own + i] + sib[i]
        hand_over(
            mid.at[i], low.at[which1], low_send.at[i], low_recv.at[which1],
            at(2 * upper + block // 2, high_bits[i], block % 2),
        )
    spot2 = block % 2
    for i in range(2):
        gain2[i] = gains_of(mid[i])
        hand_over(
            gain2.at[i], home2.at[spot2], g2_send.at[i], g2_recv.at[spot2],
            16 * (z // 2) + 8 * (block // 2) + high_bits[i],
        )

    for i in range(4):
        arrived(home3.at[i], g3_recv.at[i])
        out_ref[i:i + 1, :] = home3[i]

    for i in range(2 * NX):
        arrived(part_x.at[i], px_recv.at[i])
    total_x = part_x[0]
    for i in range(1, 2 * NX):
        total_x = total_x + part_x[i]
    scores = -total_x[0:8] / jnp.sqrt(total_x[8:16] + penalty)
    out_ref[8:12, :] = scores[0:4]
    out_ref[12:14, :] = jnp.where(z < NZ // 2, scores[4:6], scores[6:8])

    for i in range(2):
        arrived(low.at[i], low_recv.at[i])
    last = gains_of(low[0] + low[1])
    out_ref[6:7, :] = last
    for i in range(2):
        arrived(home2.at[i], g2_recv.at[i])
        out_ref[4 + i:5 + i, :] = home2[i]

    for leave in leaving:
        leave()


def spread(all_ref, one_ref, two_ref, three_ref, child_out):
    for first, ref in ((0, three_ref), (4, two_ref), (6, one_ref)):
        for i in range(ref.shape[0] // 2):
            ref[2 * i:2 * i + 1, :] = all_ref[first + i:first + i + 1, 0:BINS]
            ref[2 * i + 1:2 * i + 2, :] = all_ref[first + i:first + i + 1, BINS:2 * BINS]
    for level in range(LEVELS):
        child_out[level, 0] = all_ref[8 + 2 * level:10 + 2 * level, :]


def on_device(gradients, hessians, bin_words, children, split_feature, split_bin):
    dma = pltpu.SemaphoreType.DMA
    vmem = pl.BlockSpec(memory_space=pltpu.VMEM)
    together = pl.pallas_call(
        kernel,
        out_shape=pltpu.VMEM((16, 128), F32),
        in_specs=[pl.BlockSpec(memory_space=pl.ANY)] * 6,
        out_specs=vmem,
        scratch_shapes=[
            pltpu.SMEM((SPLITS,), jnp.int32),
            pltpu.SMEM((SPLITS,), jnp.int32),
            pltpu.VMEM((ROW_DEV, OUT), BF16),
            pltpu.VMEM((ROW_DEV,), BF16),
            pltpu.VMEM((32, ROW_DEV), jnp.int32),
            pltpu.VMEM((LEVELS, ROW_DEV), jnp.int32),
            pltpu.VMEM((NZ, PIECE, SLOTS), BF16),
            pltpu.VMEM((NZ, 1, SLOTS), F32),
            pltpu.VMEM((NZ - 1, PIECE, SLOTS), BF16),
            pltpu.VMEM((NZ, 1, SLOTS), F32),
            pltpu.VMEM((NY - 1, NZ, GOES_Y, SLOTS), BF16),
            pltpu.VMEM((NY - 1, NZ, 1, SLOTS), F32),
            pltpu.VMEM((NY, NZ, HALF, SLOTS), BF16),
            pltpu.VMEM((16, NZ * SLOTS), F32),
            pltpu.VMEM((8, KEEP, 128), F32),
            pltpu.VMEM((4, KEEP, 128), F32),
            pltpu.VMEM((4, KEEP, 128), F32),
            pltpu.VMEM((2, KEEP, 128), F32),
            pltpu.VMEM((2, KEEP, 128), F32),
            pltpu.VMEM((2, KEEP, 128), F32),
            pltpu.VMEM((4, 1, 128), F32),
            pltpu.VMEM((4, 1, 128), F32),
            pltpu.VMEM((2, 1, 128), F32),
            pltpu.VMEM((2, 1, 128), F32),
            pltpu.VMEM((NY, 16, 128), F32),
            pltpu.VMEM((NY, 16, 128), F32),
            pltpu.VMEM((16, 128), F32),
            pltpu.VMEM((NZ, 16, 128), F32),
            pltpu.VMEM((16, 128), F32),
            pltpu.VMEM((2 * NX, 16, 128), F32),
            dma((6,)), dma((NZ,)), dma((NZ,)), dma, dma, dma((NY,)), dma((NY - 1, 4)),
            dma((NY,)), dma((NY - 1,)), dma((2,)), dma((NY, 2)),
            dma((4,)), dma((4,)), dma((2,)), dma((2,)),
            dma((2,)), dma((2,)), dma((4,)), dma((4,)), dma((2,)), dma((2,)),
            dma((NY,)), dma((NY,)), dma((NZ,)), dma((NZ,)), dma((2 * NX,)), dma((2 * NX,)),
        ],
        compiler_params=pltpu.CompilerParams(collective_id=0, has_side_effects=True),
    )(split_feature, split_bin, gradients, hessians, bin_words, children)
    together = pltpu.with_memory_space_constraint(together, pltpu.VMEM)
    return pl.pallas_call(
        spread,
        out_shape=(
            jax.ShapeDtypeStruct((2, BINS), F32),
            jax.ShapeDtypeStruct((4, BINS), F32),
            jax.ShapeDtypeStruct((8, BINS), F32),
            jax.ShapeDtypeStruct((LEVELS, 1, 2, OUT), F32),
        ),
        in_specs=[vmem],
        out_specs=(vmem,) * 4,
    )(together)


def solution(mesh):
    placed = (P("rows", None), P("rows"), P("feat", "rows"), P(None, "rows"), P(), P())
    return jax.shard_map(
        on_device,
        mesh=mesh,
        in_specs=placed,
        out_specs=(
            P("rows", "feat"),
            P("rows", "feat"),
            P("rows", "feat"),
            P(None, "rows", None, None),
        ),
        check_vma=False,
    )
```

```python
import jax
import jax.numpy as jnp
from jax import lax
from jax.experimental import pallas as pl
from jax.experimental.pallas import tpu as pltpu
from jax.sharding import PartitionSpec as P

BINS = 64
OUT = 128
LEVELS = 3
SPLITS = 14
ROW_DEV = 512
SLOTS = 128
NY, NZ, NX = 4, 8, 4
HALF = OUT // 2
PIECE = HALF + 64
GOES_Y = HALF + 16
KEEP = OUT + 8
MESH = pl.DeviceIdType.MESH
F32 = jnp.float32
BF16 = jnp.bfloat16

penalty = 1.0
DIRECT = (0, 1, 2, 3)
NEAR = (0, 1, 7, 2, 6, 4, 3, 5)


def block_of(y, upper):
    block = 2 * (((y + 1) // 2) % 2) + y // 2
    return block + upper * (3 - 2 * block)


def nt_dot(left, right):
    return lax.dot_general(left, right, (((1,), (1,)), ((), ())), preferred_element_type=F32)


def ones_where(condition):
    return condition.astype(F32).astype(BF16)


def gains_of(left):
    total = jnp.broadcast_to(left[:, 127:128], left.shape)
    right = total - left

    def term(part):
        square = part[:OUT] * part[:OUT]
        return jnp.sum(square, axis=0, keepdims=True) / (part[OUT:OUT + 1] + penalty)

    return (term(left) + term(right) - term(total)) / OUT


def kernel(
    split_feature_any, split_bin_any, grad_any, hess_any, word_any, child_any,
    out_ref,
    split_feature, split_bin, grad_ref, hess_ref, word_ref, child_ref,
    sent, sent_h, got_z, got_h, got_y, got_yh, got_x, codes_here,
    acc, half, deep, sib, mid, low,
    gain3, home3, gain2, home2, part, part_y, mine_z, part_z, mine_x, part_x,
    in_sem, z_send, z_recv, zh_send, zh_recv, y_send, y_recv, yh_send, yh_recv,
    x_send, x_recv, core_send, core_recv, sib_send, sib_recv,
    low_send, low_recv, g3_send, g3_recv, g2_send, g2_recv,
    py_send, py_recv, pz_send, pz_recv, px_send, px_recv,
):
    row = lax.axis_index("rows")
    x = lax.axis_index("feat")
    core = row % 2
    z = (row // 2) % NZ
    y = row // 16
    upper = z // 4
    block = block_of(y, upper)
    kind = (z + upper) % 2
    own = 2 * kind
    other = 2 - own
    leaving = []

    def at(y_to, z_to, core_to):
        return y_to * 16 + z_to * 2 + core_to

    def remote(src, dst, send, recv, row_to, x_to=None):
        return pltpu.make_async_remote_copy(
            src_ref=src, dst_ref=dst, send_sem=send, recv_sem=recv,
            device_id=(row_to, x if x_to is None else x_to), device_id_type=MESH,
        )

    def arrived(ref, sem):
        pltpu.make_async_copy(ref, ref, sem).wait()

    def left_with(ref, sem):
        leaving.append(lambda: arrived(ref, sem))

    inputs = [
        pltpu.make_async_copy(src, dst, in_sem.at[i])
        for i, (src, dst) in enumerate((
            (child_any, child_ref), (hess_any, hess_ref), (word_any, word_ref),
            (grad_any, grad_ref), (split_feature_any, split_feature), (split_bin_any, split_bin),
        ))
    ]
    for copy in inputs:
        copy.start()

    barrier = pltpu.get_barrier_semaphore()

    def greet(row_to, x_to):
        pl.semaphore_signal(barrier, inc=1, device_id=(row_to, x_to), device_id_type=MESH)

    for step in (4, 3, 5, 2, 6, 1, 7):
        greet(at(y, (z + step) % NZ, core), x)
    for step in (2, 1, 3):
        greet(at((y + step) % NY, z, core), x)
    for step in (2, 1, 3):
        for side in (1, NX - 1):
            greet(at((y + step) % NY, z, core), (x + side) % NX)
    for step in range(1, 2 * NX):
        greet(at(y, z, (core + step) % 2), (x + step // 2) % NX)
    for copy in inputs:
        copy.wait()

    child = child_ref[...]
    node1 = child[0:1]
    node2 = node1 * 2 + child[1:2]
    node3 = node2 * 2 + child[2:3]
    at_node = (lax.broadcasted_iota(jnp.int32, (8, ROW_DEV), 0) == node3).astype(F32)
    upto = ones_where(
        lax.broadcasted_iota(jnp.int32, (ROW_DEV, ROW_DEV), 0)
        <= lax.broadcasted_iota(jnp.int32, (ROW_DEV, ROW_DEV), 1)
    )
    running = jnp.dot(at_node.astype(BF16), upto, preferred_element_type=F32)
    rank = jnp.sum(at_node * running, axis=0, keepdims=True).astype(jnp.int32) - 1
    slot = node3 * SLOTS + rank

    hess = hess_ref[...].reshape(1, ROW_DEV).astype(F32)
    outputs_all = grad_ref[...].astype(F32).T
    outputs_half = jnp.where(x % 2 == 0, outputs_all[:HALF], outputs_all[HALF:]).astype(BF16)
    words = word_ref[...]
    natural = jnp.concatenate(
        [jnp.bitwise_and(words, 63), jnp.bitwise_and(jnp.right_shift(words, 6), 63)], 0
    ).astype(F32).astype(BF16)
    spot64 = lax.broadcasted_iota(jnp.int32, (64, 1), 0)
    source64 = (
        32 * jnp.bitwise_and(jnp.right_shift(spot64, 3), 1)
        + 16 * jnp.right_shift(spot64, 5)
        + 2 * jnp.bitwise_and(spot64, 7)
        + jnp.bitwise_and(jnp.right_shift(spot64, 4), 1)
    )
    moved = ones_where(lax.broadcasted_iota(jnp.int32, (64, 64), 1) == source64)
    code_rows = jnp.dot(moved, natural, preferred_element_type=F32).astype(BF16)
    hess_tile = jnp.concatenate([hess, jnp.zeros((15, ROW_DEV), F32)], 0).astype(BF16)
    packed = jnp.concatenate([outputs_half, code_rows, hess_tile], 0)
    for pair in range(NZ // 2):
        wanted = lax.broadcasted_iota(jnp.int32, (2 * SLOTS, ROW_DEV), 0) + pair * 2 * SLOTS
        chosen = nt_dot(packed, ones_where(wanted == slot))
        for side in range(2):
            lanes = slice(side * SLOTS, (side + 1) * SLOTS)
            sent[2 * pair + side] = chosen[:PIECE, lanes].astype(BF16)
            sent_h[2 * pair + side] = chosen[PIECE:PIECE + 1, lanes]
    got_h[0] = sent_h[z]

    pl.semaphore_wait(barrier, (NZ - 1) + 3 * (NY - 1) + (2 * NX - 1))
    for step in (1, 7, 4, 2, 6, 3, 5):
        z_to = (z + step) % NZ
        place = NEAR.index((NZ - step) % NZ)
        remote(
            sent.at[z_to], got_z.at[place - 1], z_send.at[step], z_recv.at[place], at(y, z_to, core)
        ).start()
        left_with(sent.at[step], z_send.at[step])
    for step in (1, 7, 4, 2, 6, 3, 5):
        z_to = (z + step) % NZ
        place = NEAR.index((NZ - step) % NZ)
        remote(
            sent_h.at[z_to], got_h.at[place], zh_send, zh_recv, at(y, z_to, core)
        ).start()
    left_with(got_h.at[pl.ds(1, NZ - 1)], zh_send)

    rows32 = lax.broadcasted_iota(jnp.int32, (32, 1), 0)
    yy = jnp.right_shift(rows32, 3)
    which = jnp.bitwise_and(jnp.right_shift(rows32, 1), 3)
    right_side = jnp.bitwise_and(rows32, 1)
    is_one, is_two = which == 0, which == 1
    node_row = jnp.where(
        is_one, jnp.right_shift(yy, 1), jnp.where(is_two, yy, 2 * yy + which - 2)
    )
    split_row = node_row + jnp.where(is_one, 0, jnp.where(is_two, 2, 6))
    feature_row = jnp.zeros((32, 1), jnp.int32)
    bin_row = jnp.zeros((32, 1), jnp.int32)
    for s in range(SPLITS):
        feature_row = jnp.where(split_row == s, split_feature[s], feature_row)
        bin_row = jnp.where(split_row == s, split_bin[s], bin_row)
    inner = jnp.bitwise_and(feature_row, 63)
    place = (
        32 * jnp.right_shift(inner, 5)
        + 16 * jnp.bitwise_and(jnp.right_shift(inner, 1), 1)
        + 8 * jnp.bitwise_and(inner, 1)
        + jnp.bitwise_and(jnp.right_shift(inner, 2), 7)
    )
    panel_row = jnp.right_shift(feature_row, 6)
    spot = ones_where(lax.broadcasted_iota(jnp.int32, (32, 64), 1) == place)
    code_row = jnp.dot(spot, code_rows, preferred_element_type=F32).astype(jnp.int32)
    node_here = jnp.where(is_one, node1, jnp.where(is_two, node2, node3))
    goes_right = (code_row > bin_row).astype(jnp.int32)
    wanted_row = (node_here == node_row) & (panel_row == x) & (goes_right == right_side)
    wanted_row = wanted_row.astype(F32)
    sums = jnp.dot(wanted_row.astype(BF16), grad_ref[...], preferred_element_type=F32)
    sums_h = jnp.sum(wanted_row * hess, axis=1, keepdims=True)
    for y_to in range(NY):
        part[y_to, 0:8] = sums[8 * y_to:8 * y_to + 8]
        part[y_to, 8:16] = jnp.broadcast_to(sums_h[8 * y_to:8 * y_to + 8], (8, OUT))
    for step in range(1, NY):
        y_to = (y + step) % NY
        remote(
            part.at[y_to], part_y.at[y], py_send.at[step], py_recv.at[y], at(y_to, z, core)
        ).start()
        left_with(part.at[step], py_send.at[step])
    pltpu.make_async_copy(part.at[y], part_y.at[y], py_recv.at[y]).start()

    def piece(place):
        return sent.at[z] if place == 0 else got_z.at[place - 1]

    def to_x(src, offset, place, y_step=0):
        step = 1 - 2 * (place % 2)
        late = int(place >= NZ // 2)
        remote(
            src, got_x.at[offset, place], x_send.at[place % 2], x_recv.at[offset, late],
            at((y + y_step) % NY, z, core), (x + step) % NX,
        ).start()

    def from_z(group):
        for place in (2 * group, 2 * group + 1):
            if place:
                arrived(got_z.at[place - 1], z_recv.at[place])
            here = piece(place)
            for step in (1, 3, 2):
                remote(
                    here.at[pl.ds(0, HALF)], got_y.at[NY - step - 1, place, pl.ds(0, HALF)],
                    y_send.at[step], y_recv.at[NY - step - 1, group],
                    at((y + step) % NY, z, core),
                ).start()
            for step in (1, 3, 2):
                y_to = (y + step) % NY
                start = pl.multiple_of(HALF + 16 * block_of(y_to, upper), 16)
                remote(
                    here.at[pl.ds(start, 16)], got_y.at[NY - step - 1, place, pl.ds(HALF, 16)],
                    y_send.at[step], y_recv.at[NY - step - 1, group], at(y_to, z, core),
                ).start()
            for step in (2, 1, 3, 0) if group in DIRECT else (0,):
                to_x(here.at[pl.ds(0, HALF)], (NY - step) % NY, place, step)

    def from_y(offset, group):
        arrived(got_y.at[offset - 1, pl.ds(2 * group, 2)], y_recv.at[offset - 1, group])
        for place in (2 * group, 2 * group + 1) if group not in DIRECT else ():
            to_x(got_y.at[offset - 1, place, pl.ds(0, HALF)], offset, place)

    bins = lax.broadcasted_iota(jnp.int32, (BINS, 1), 0).astype(F32)

    def add_rows(offset, first=False, after=None, places=range(NZ)):
        for late in range(places[0] // 4, places[-1] // 4 + 1):
            arrived(got_x.at[offset, pl.ds(4 * late, 4)], x_recv.at[offset, late])
        if offset == 0:
            pieces = [piece(i) for i in places]
            start = pl.multiple_of(HALF + 16 * block, 16)
            kept = [ref[0:HALF, :] for ref in pieces]
            codes = [ref[pl.ds(start, 16), :] for ref in pieces]
            weights = [got_h[i] for i in places]
        else:
            if places[0] == 0:
                arrived(got_yh.at[offset - 1], yh_recv.at[offset - 1])
            kept = [got_y[offset - 1, i, 0:HALF, :] for i in places]
            codes = [got_y[offset - 1, i, HALF:GOES_Y, :] for i in places]
            weights = [got_yh[offset - 1, i] for i in places]
        tile = jnp.concatenate(
            [jnp.concatenate(weights, 1), jnp.zeros((15, len(places) * SLOTS), F32)], 0
        ).astype(BF16)
        values = jnp.concatenate([
            jnp.concatenate(kept, 1),
            jnp.concatenate([got_x[offset, i] for i in places], 1),
            tile,
        ], 0)
        codes_here[:, 0:len(places) * SLOTS] = jnp.concatenate(codes, 1).astype(F32)
        for turn, (core_to, base) in enumerate(
            ((1 - core, other), (1 - core, own), (core, other), (core, own))
        ):
            masks = []
            for i in range(2):
                high = (2 * (base + i) + 5 * core_to) % 8
                for line in (high, 8 + high):
                    masks.append(ones_where(codes_here[pl.ds(line, 1), 0:len(places) * SLOTS] <= bins))
            found = nt_dot(values, jnp.concatenate(masks, 0))
            for i in range(2):
                new = found[:KEEP, 128 * i:128 * i + 128]
                if first:
                    acc[4 * core_to + base + i] = new
                else:
                    acc[4 * core_to + base + i] += new
            if after is not None:
                after(turn)

    buddy = at(y, z, 1 - core)

    def to_buddy(turn):
        if turn < 2:
            base = (other, own)[turn]
            for i in range(2):
                remote(
                    acc.at[4 * (1 - core) + base + i], half.at[base + i],
                    core_send.at[2 * turn + i], core_recv.at[2 * turn + i], buddy,
                ).start()
                left_with(half.at[0], core_send.at[2 * turn + i])

    from_z(0)
    from_z(1)
    from_z(2)
    from_z(3)
    arrived(got_h.at[pl.ds(1, NZ - 1)], zh_recv)
    for step in range(1, NY):
        remote(
            got_h, got_yh.at[NY - step - 1], yh_send.at[step], yh_recv.at[NY - step - 1],
            at((y + step) % NY, z, core),
        ).start()
        left_with(got_h, yh_send.at[step])
    for y_from in range(NY):
        arrived(part_y.at[y_from], py_recv.at[y_from])
    mine_z[...] = (part_y[0] + part_y[1]) + (part_y[2] + part_y[3])
    for step in range(1, NZ):
        remote(
            mine_z, part_z.at[z], pz_send.at[step], pz_recv.at[z], at(y, (z + step) % NZ, core)
        ).start()
        left_with(mine_z, pz_send.at[step])
    pltpu.make_async_copy(mine_z, part_z.at[z], pz_recv.at[z]).start()
    add_rows(0, first=True, places=range(0, 8))
    from_y(1, 0)
    from_y(1, 1)
    from_y(1, 2)
    from_y(1, 3)
    add_rows(1, places=range(0, 8))
    from_y(3, 0)
    from_y(3, 1)
    from_y(3, 2)
    from_y(3, 3)
    add_rows(3, places=range(0, 8))
    from_y(2, 0)
    from_y(2, 1)
    add_rows(2, places=range(0, 4))
    from_y(2, 2)
    from_y(2, 3)
    add_rows(2, places=range(4, 8), after=to_buddy)
    for step in range(1, NY):
        left_with(got_y.at[0], y_send.at[step])
    for side in range(2):
        left_with(got_x.at[pl.ds(0, 2)], x_send.at[side])

    sibling = at(y, z + 1 - 2 * (z % 2), core)
    for i in range(2):
        arrived(half.at[other + i], core_recv.at[i])
        deep[other + i] = acc[4 * core + other + i] + half[other + i]
        remote(deep.at[other + i], sib.at[i], sib_send.at[i], sib_recv.at[i], sibling).start()
        left_with(sib.at[i], sib_send.at[i])
    for i in range(2):
        arrived(half.at[own + i], core_recv.at[2 + i])
        deep[own + i] = acc[4 * core + own + i] + half[own + i]

    def hand_over(src, dst, send, recv, row_to):
        @pl.when(row_to != row)
        def _():
            remote(src, dst, send, recv, row_to).start()

        @pl.when(row_to == row)
        def _():
            pltpu.make_async_copy(src, dst, recv).start()

        def leave():
            @pl.when(row_to != row)
            def _():
                arrived(src, send)

        leaving.append(leave)

    spot3 = 2 * core + block % 2
    for i in range(4):
        gain3[i] = gains_of(deep[i])
    for i in range(4):
        row_to = 8 * z + 4 * (block // 2) + (i + 2 * core) % 4
        hand_over(gain3.at[i], home3.at[spot3], g3_send.at[i], g3_recv.at[spot3], row_to)

    for z_from in range(NZ):
        arrived(part_z.at[z_from], pz_recv.at[z_from])
    total_z = part_z[0]
    for z_from in range(1, NZ):
        total_z = total_z + part_z[z_from]
    mine_x[...] = total_z
    here = 2 * x + core
    for step in range(1, 2 * NX):
        remote(
            mine_x, part_x.at[here], px_send.at[step], px_recv.at[here],
            at(y, z, (core + step) % 2), (x + step // 2) % NX,
        ).start()
        left_with(mine_x, px_send.at[step])
    pltpu.make_async_copy(mine_x, part_x.at[here], px_recv.at[here]).start()

    high_bits = [(2 * (own + i) + 5 * core) % 8 for i in range(2)]
    which1 = (z // 2) % 2
    for i in range(2):
        arrived(sib.at[i], sib_recv.at[i])
        mid[i] = deep[own + i] + sib[i]
        hand_over(
            mid.at[i], low.at[which1], low_send.at[i], low_recv.at[which1],
            at(2 * upper + block // 2, high_bits[i], block % 2),
        )
    spot2 = block % 2
    for i in range(2):
        gain2[i] = gains_of(mid[i])
        hand_over(
            gain2.at[i], home2.at[spot2], g2_send.at[i], g2_recv.at[spot2],
            16 * (z // 2) + 8 * (block // 2) + high_bits[i],
        )

    for i in range(4):
        arrived(home3.at[i], g3_recv.at[i])
        out_ref[i:i + 1, :] = home3[i]

    for i in range(2 * NX):
        arrived(part_x.at[i], px_recv.at[i])
    total_x = part_x[0]
    for i in range(1, 2 * NX):
        total_x = total_x + part_x[i]
    scores = -total_x[0:8] / jnp.sqrt(total_x[8:16] + penalty)
    out_ref[8:12, :] = scores[0:4]
    out_ref[12:14, :] = jnp.where(z < NZ // 2, scores[4:6], scores[6:8])

    for i in range(2):
        arrived(low.at[i], low_recv.at[i])
    last = gains_of(low[0] + low[1])
    out_ref[6:7, :] = last
    for i in range(2):
        arrived(home2.at[i], g2_recv.at[i])
        out_ref[4 + i:5 + i, :] = home2[i]

    for leave in leaving:
        leave()


def spread(all_ref, one_ref, two_ref, three_ref, child_out):
    for first, ref in ((0, three_ref), (4, two_ref), (6, one_ref)):
        for i in range(ref.shape[0] // 2):
            ref[2 * i:2 * i + 1, :] = all_ref[first + i:first + i + 1, 0:BINS]
            ref[2 * i + 1:2 * i + 2, :] = all_ref[first + i:first + i + 1, BINS:2 * BINS]
    for level in range(LEVELS):
        child_out[level, 0] = all_ref[8 + 2 * level:10 + 2 * level, :]


def on_device(gradients, hessians, bin_words, children, split_feature, split_bin):
    dma = pltpu.SemaphoreType.DMA
    vmem = pl.BlockSpec(memory_space=pltpu.VMEM)
    together = pl.pallas_call(
        kernel,
        out_shape=pltpu.VMEM((16, 128), F32),
        in_specs=[pl.BlockSpec(memory_space=pl.ANY)] * 6,
        out_specs=vmem,
        scratch_shapes=[
            pltpu.SMEM((SPLITS,), jnp.int32),
            pltpu.SMEM((SPLITS,), jnp.int32),
            pltpu.VMEM((ROW_DEV, OUT), BF16),
            pltpu.VMEM((ROW_DEV,), BF16),
            pltpu.VMEM((32, ROW_DEV), jnp.int32),
            pltpu.VMEM((LEVELS, ROW_DEV), jnp.int32),
            pltpu.VMEM((NZ, PIECE, SLOTS), BF16),
            pltpu.VMEM((NZ, 1, SLOTS), F32),
            pltpu.VMEM((NZ - 1, PIECE, SLOTS), BF16),
            pltpu.VMEM((NZ, 1, SLOTS), F32),
            pltpu.VMEM((NY - 1, NZ, GOES_Y, SLOTS), BF16),
            pltpu.VMEM((NY - 1, NZ, 1, SLOTS), F32),
            pltpu.VMEM((NY, NZ, HALF, SLOTS), BF16),
            pltpu.VMEM((16, NZ * SLOTS), F32),
            pltpu.VMEM((8, KEEP, 128), F32),
            pltpu.VMEM((4, KEEP, 128), F32),
            pltpu.VMEM((4, KEEP, 128), F32),
            pltpu.VMEM((2, KEEP, 128), F32),
            pltpu.VMEM((2, KEEP, 128), F32),
            pltpu.VMEM((2, KEEP, 128), F32),
            pltpu.VMEM((4, 1, 128), F32),
            pltpu.VMEM((4, 1, 128), F32),
            pltpu.VMEM((2, 1, 128), F32),
            pltpu.VMEM((2, 1, 128), F32),
            pltpu.VMEM((NY, 16, 128), F32),
            pltpu.VMEM((NY, 16, 128), F32),
            pltpu.VMEM((16, 128), F32),
            pltpu.VMEM((NZ, 16, 128), F32),
            pltpu.VMEM((16, 128), F32),
            pltpu.VMEM((2 * NX, 16, 128), F32),
            dma((6,)), dma((NZ,)), dma((NZ,)), dma, dma, dma((NY,)), dma((NY - 1, 4)),
            dma((NY,)), dma((NY - 1,)), dma((2,)), dma((NY, 2)),
            dma((4,)), dma((4,)), dma((2,)), dma((2,)),
            dma((2,)), dma((2,)), dma((4,)), dma((4,)), dma((2,)), dma((2,)),
            dma((NY,)), dma((NY,)), dma((NZ,)), dma((NZ,)), dma((2 * NX,)), dma((2 * NX,)),
        ],
        compiler_params=pltpu.CompilerParams(collective_id=0, has_side_effects=True),
    )(split_feature, split_bin, gradients, hessians, bin_words, children)
    together = pltpu.with_memory_space_constraint(together, pltpu.VMEM)
    return pl.pallas_call(
        spread,
        out_shape=(
            jax.ShapeDtypeStruct((2, BINS), F32),
            jax.ShapeDtypeStruct((4, BINS), F32),
            jax.ShapeDtypeStruct((8, BINS), F32),
            jax.ShapeDtypeStruct((LEVELS, 1, 2, OUT), F32),
        ),
        in_specs=[vmem],
        out_specs=(vmem,) * 4,
    )(together)


def solution(mesh):
    placed = (P("rows", None), P("rows"), P("feat", "rows"), P(None, "rows"), P(), P())
    return jax.shard_map(
        on_device,
        mesh=mesh,
        in_specs=placed,
        out_specs=(
            P("rows", "feat"),
            P("rows", "feat"),
            P("rows", "feat"),
            P(None, "rows", None, None),
        ),
        check_vma=False,
    )
```
